256 devices in a mesh: rows: 8 (over y, z_hi), cols: 32 (over x, z_lo, core).
Axes of the slice: x: 4, y: 4, z: 8 (z_hi: 2, z_lo: 4; z = z_hi * 4 + z_lo), core: 2. Of those that a mesh axis runs over, the one named last changes fastest.
Arguments:
- covariance: float32 [8192, 8192], P('rows', 'cols'), may hold values from -6 to 6
- zonal: float32 [64, 128, 128], P('rows'), may hold values from -0.5 to 0.5
- stencil: float32 [64, 3, 128], P('rows'), may hold values from -0.5 to 1.1, as said below
Outputs:
- lagged: float32 [8192, 8192], P('rows', 'cols')
The draws below stay inside these ranges and needn't reach their ends.
Inputs may be any that keep to these rules, and one draw needn't show every extreme that they name: `stencil`: component 0 lies in 0.7 to 1.1, components 1 and 2 in -0.5 to 0.5.
All inputs are finite; a program needn't handle non-finite values.
Results may differ from the reference program's by a relative error of at most 0.0003.
Values sent between devices are 32-bit elements; how exact they have to be, the bound alone decides.
A program may use at most 64 MiB of HBM per device.

```python
import jax
import jax.numpy as jnp
from jax import lax

LON = 128
STEPS = 3
LAGS = 3
NLAT = 64
NSTATE = 8192


def draw_stencil(key, part):
    first, second = jax.random.split(jax.random.fold_in(key, 11))
    middle = jax.random.uniform(first, (NLAT, 1, LON), jnp.float32, 0.7, 1.1)
    sides = jax.random.uniform(second, (NLAT, 2, LON), jnp.float32, -0.5, 0.5)
    return jnp.concatenate([middle, sides], axis=1)


def level_of(rng, extent, cuts, low, largest):
    level = 1.0
    for dim, shards_of in cuts:
        steps = jax.random.uniform(jax.random.fold_in(jax.random.fold_in(rng, 6), dim), (shards_of,), jnp.float32, low / len(cuts), largest / len(cuts))
        level = level * jnp.repeat(jnp.exp(steps), extent[dim] // shards_of).reshape((-1,) + (1,) * (len(extent) - 1 - dim))
    return level


def scatter_about(own_key, extent, deviation, reach, cuts=(), held_as=jnp.bfloat16):
    result = deviation * jax.random.normal(own_key, extent, jnp.float32)
    if cuts:
        result = result * level_of(own_key, extent, cuts, -0.22, 0.18)
    return jnp.clip(result, -reach, reach).astype(held_as)


def setup_inputs(seed: int = 0) -> dict:
    splits = jax.random.split(jax.random.key(seed), 4)
    covariance = scatter_about(splits[0], (NSTATE, NSTATE), 1.0, 6.0, ((0, 8), (1, 32)), jnp.float32)
    zonal = scatter_about(splits[1], (NLAT, LON, LON), LON ** -0.5, 0.5, ((0, 8),), jnp.float32)
    stencil = draw_stencil(jax.random.fold_in(splits[3], 71), 0)
    return {"covariance": covariance, "zonal": zonal, "stencil": stencil}


def left_apply(matrix, zonal, stencil):
    latitudes = zonal.shape[0]
    longitudes = zonal.shape[1]
    blocks = matrix.reshape(latitudes, longitudes, matrix.shape[1])

    def one_latitude(lat):
        north_lat = jnp.minimum(lat + 1, latitudes - 1).astype(jnp.int32)
        south_lat = jnp.maximum(lat - 1, 0).astype(jnp.int32)
        north_flag = jnp.where(lat + 1 < latitudes, 1.0, 0.0).astype(matrix.dtype)
        south_flag = jnp.where(lat > 0, 1.0, 0.0).astype(matrix.dtype)
        own = lax.dynamic_index_in_dim(blocks, lat, 0, False)
        north = lax.dynamic_index_in_dim(blocks, north_lat, 0, False) * north_flag
        south = lax.dynamic_index_in_dim(blocks, south_lat, 0, False) * south_flag
        coeffs = lax.dynamic_index_in_dim(stencil, lat, 0, False)
        mixed = coeffs[0][:, None] * own + coeffs[1][:, None] * north + coeffs[2][:, None] * south
        matrix_lat = lax.dynamic_index_in_dim(zonal, lat, 0, False)
        return jnp.dot(matrix_lat, mixed, preferred_element_type=jnp.float32, precision=lax.Precision.HIGHEST).astype(matrix.dtype)

    turned = lax.map(one_latitude, jnp.arange(latitudes, dtype=jnp.int32))
    return turned.reshape(matrix.shape)


def reference(covariance, zonal, stencil):
    current = covariance
    for repeat in range(STEPS):
        current = left_apply(current, zonal, stencil)
    current = current.T
    for repeat in range(STEPS):
        current = left_apply(current, zonal, stencil)
    for repeat in range(LAGS):
        current = left_apply(current, zonal, stencil)
    return current
```

```python
import jax
import jax.numpy as jnp
from jax import lax
from jax.experimental import pallas as pl
from jax.experimental.pallas import tpu as pltpu
from jax.sharding import PartitionSpec as P

MESH = pl.DeviceIdType.MESH
N = 128
F32, BF16 = jnp.float32, jnp.bfloat16


def div(a, b):
    return lax.div(a, jnp.int32(b))


def rem(a, b):
    return lax.rem(a, jnp.int32(b))


def device(x, y, z, core):
    return (y * 2 + div(z, 4), x * 8 + rem(z, 4) * 2 + core)


def rows(first, count):
    return pl.ds(pl.multiple_of(first * N, N), count * N)


def kernel(cov, zonal, stencil, out, op, b_hi, b_lo, x1, x2, x3, ya, yb, ts, es,
           e_send, e_recv, o_send, o_recv, h_send, h_recv, t_send, t_recv, f_send, g_send, g_recv):
    row, col = lax.axis_index("rows"), lax.axis_index("cols")
    y, zh = div(row, 2), rem(row, 2)
    x, zl, core = div(col, 8), div(rem(col, 8), 2), rem(col, 2)
    z = zh * 4 + zl
    me16 = z * 2 + core
    partner = (row + 1 - 2 * zh, col)
    piece = x * 2 + core
    other = 1 - zh
    edge_chip = (zl == 0) | (zl == 3)
    diagonal = x == y
    clat = zl * 4 + core * 2 + zh

    def remote(src, dst, send, recv, dev):
        return pltpu.make_async_remote_copy(
            src_ref=src, dst_ref=dst, send_sem=send, recv_sem=recv, device_id=dev, device_id_type=MESH)

    for i in range(8):
        op[2 + 8 * zh + i, 0:N, :] = zonal[i]
        op[2 + 8 * zh + i, N:N + 3, :] = stencil[i]

    @pl.when(y == 0)
    def _():
        op[0:2] = jnp.zeros((2, N + 8, N), F32)
        for ref in (x1, x2, x3):
            ref[0:3 * N, :] = jnp.zeros((3 * N, N), F32)

    @pl.when(y == 3)
    def _():
        op[18:20] = jnp.zeros((2, N + 8, N), F32)
        for ref in (x1, x2, x3):
            ref[19 * N:22 * N, :] = jnp.zeros((3 * N, N), F32)

    barrier = pltpu.get_barrier_semaphore()

    def greet(dev):
        pl.semaphore_signal(barrier, inc=1, device_id=dev, device_id_type=MESH)

    greet(partner)
    near = jnp.where(zh == 0, jnp.where(zl < 2, 7, 4), jnp.where(zl < 2, 3, 0))
    greet(device(x, y, near, core))

    def greet_group(k, c):
        q = rem(piece + k, 8)
        greet(device(div(q, 2), y, z, rem(q, 2)))
        return c

    lax.fori_loop(1, 8, greet_group, 0)

    @pl.when(y > 0)
    def _():
        greet(device(x, y - 1, z, core))

    @pl.when(y < 3)
    def _():
        greet(device(x, y + 1, z, core))

    @pl.when(diagonal)
    def _():
        def same(k, c):
            d = rem(me16 + k, 16)
            greet(device(x, y, div(d, 2), rem(d, 2)))
            return c

        lax.fori_loop(1, 16, same, 0)

        def relayed(j, c):
            greet(device(x, rem(x + 1 + div(j, 8), 4), rem(j, 8), 1 - core))
            return c

        lax.fori_loop(0, 24, relayed, 0)

    @pl.when(jnp.logical_not(diagonal))
    def _():
        def direct(k, c):
            greet(device(y, x, k, core))
            return c

        lax.fori_loop(0, 8, direct, 0)
        greet(device(y, y, z, core))

    writes = (1 + 7 + jnp.where(edge_chip, 2, 0) + jnp.where(y > 0, 1, 0) + jnp.where(y < 3, 1, 0)
              + jnp.where(diagonal, 15 + 3, 16))
    pl.semaphore_wait(barrier, writes)

    theirs = pl.ds(pl.multiple_of(other * N, N), N)
    mine = pl.ds(pl.multiple_of(zh * N, N), N)
    swap_edge = remote(cov.at[rows(zh * 5, 3), theirs], x1.at[rows(3 + zh * 13, 3)],
                       e_send.at[0], e_recv.at[0], partner)
    swap_rest = remote(cov.at[rows(other * 3, 5), theirs], x1.at[rows(6 + zh * 5, 5)],
                       e_send.at[1], e_recv.at[1], partner)

    @pl.when(edge_chip)
    def _():
        for far in range(2):
            to = jnp.where(zl == 3, rem(z + 1 + far, 8), rem(z + 7 - far, 8))
            slot = 2 + 8 * zh + piece
            remote(op.at[slot], op.at[slot], o_send.at[far], o_recv.at[piece], device(x, y, to, core)).start()

    swap_edge.start()
    swap_rest.start()

    def border(stage, side, src, dst_first):
        dev = device(x, jnp.where(side == 0, y - 1, y + 1), z, core)
        return remote(src, dst_first, h_send.at[stage * 2 + side], h_recv.at[stage * 2 + side], dev)

    def has(side):
        return jnp.where(side == 0, y > 0, y < 3)

    @pl.when(has(zh))
    def _():
        border(0, zh, cov.at[rows(zh * 5, 3), mine], x1.at[rows(19 - 19 * zh, 3)]).start()

    x1[rows(3 + 8 * zh, 8), :] = cov[:, mine]

    slot = 2 + 8 * other + piece
    remote(op.at[slot], op.at[slot], o_send.at[0], o_recv.at[piece], partner).wait_recv()

    def share(k, c):
        q = rem(piece + k, 8)
        remote(op.at[slot], op.at[slot], o_send.at[1 + k], o_recv.at[piece], device(div(q, 2), y, z, rem(q, 2))).start()
        return c

    lax.fori_loop(1, 8, share, 0)

    def build(l, c):
        z_mat = op[l, 0:N, :]
        for part, comp in enumerate((2, 0, 1)):
            scaled = z_mat * op[l, N + comp:N + comp + 1, :]
            hi = scaled.astype(BF16)
            b_hi[l, :, part * N:(part + 1) * N] = hi
            b_lo[l, :, part * N:(part + 1) * N] = (scaled - hi.astype(F32)).astype(BF16)
        return c

    lax.fori_loop(2 + 8 * zh, 10 + 8 * zh, build, 0)

    swap_edge.wait_recv()

    @pl.when(has(other))
    def _():
        border(0, other, x1.at[rows(3 + 13 * other, 3)], x1.at[rows(19 - 19 * other, 3)]).start()

    def shared(k, c):
        q = rem(piece + k, 8)
        s = 2 + 8 * other + q
        remote(op.at[s], op.at[s], o_send.at[0], o_recv.at[q], partner).wait_recv()
        return c

    lax.fori_loop(1, 8, shared, 0)

    @pl.when(y > 0)
    def _():
        remote(op.at[pl.ds(2, 2)], op.at[pl.ds(18, 2)], o_send.at[9], o_recv.at[8],
               device(x, y - 1, z, core)).start()

    @pl.when(y < 3)
    def _():
        remote(op.at[pl.ds(16, 2)], op.at[pl.ds(0, 2)], o_send.at[10], o_recv.at[9],
               device(x, y + 1, z, core)).start()

    lax.fori_loop(2 + 8 * other, 10 + 8 * other, build, 0)

    @pl.when(y < 3)
    def _():
        remote(op.at[pl.ds(18, 2)], op.at[pl.ds(18, 2)], o_send.at[0], o_recv.at[8], partner).wait_recv()

    @pl.when(y > 0)
    def _():
        remote(op.at[pl.ds(0, 2)], op.at[pl.ds(0, 2)], o_send.at[0], o_recv.at[9], partner).wait_recv()

    lax.fori_loop(0, 2, build, 0)
    lax.fori_loop(18, 20, build, 0)

    def one(src, i):
        v = src[rows(i, 3), :]
        hi = v.astype(BF16)
        lo = (v - hi.astype(F32)).astype(BF16)
        bh = b_hi[i]
        acc = jnp.dot(bh, lo, preferred_element_type=F32)
        acc += jnp.dot(b_lo[i], hi, preferred_element_type=F32)
        return acc + jnp.dot(bh, hi, preferred_element_type=F32)

    def sweep(src, dst, first, last):
        def body(i, c):
            dst[rows(i + 1, 1), :] = one(src, i)
            return c

        lax.fori_loop(first + 2, last + 2, body, 0)

    def wait_borders(stage, ref):
        @pl.when(y < 3)
        def _():
            border(stage, 0, ref.at[rows(19, 3)], ref.at[rows(19, 3)]).wait_recv()

        @pl.when(y > 0)
        def _():
            border(stage, 1, ref.at[rows(0, 3)], ref.at[rows(0, 3)]).wait_recv()

    swap_rest.wait_recv()
    wait_borders(0, x1)
    sweep(x1, ya, -2, 18)
    sweep(ya, yb, -1, 17)

    def turn(lat, c):
        ts[lat] = one(yb, lat + 2).T
        return c

    lax.fori_loop(0, 16, turn, 0)

    def target(k):
        d = rem(me16 + k, 16)
        zt, ct = div(d, 2), rem(d, 2)
        lat = 8 * div(rem(zt, 4), 2) + 4 * rem(zt, 2) + 2 * ct + div(zt, 4)
        relay = jnp.logical_and(jnp.logical_not(diagonal), ct != core)
        dev = device(jnp.where(relay, x, y), x, zt, ct)
        slot = jnp.where(relay, 19 + rem(y + 3 - x, 4) * 8 + z, clat)
        return lat, slot, dev

    def send_block(k, c):
        lat, slot, dev = target(k)
        remote(ts.at[lat], x2.at[rows(slot + 3, 1)], t_send.at[k], t_recv.at[slot], dev).start()
        return c

    self_copy = pltpu.make_async_copy(
        ts.at[8 * div(zl, 2) + 4 * rem(zl, 2) + 2 * core + zh], x2.at[rows(clat + 3, 1)], t_recv.at[clat])

    @pl.when(diagonal)
    def _():
        self_copy.start()

    @pl.when(jnp.logical_not(diagonal))
    def _():
        send_block(0, 0)

    lax.fori_loop(1, 16, send_block, 0)

    def forward(j):
        zs = rem(j, 8)
        lat_from = rem(zs, 4) * 4 + (1 - core) * 2 + div(zs, 4)
        return remote(x2.at[rows(22 + j, 1)], x2.at[rows(lat_from + 3, 1)], f_send.at[j], t_recv.at[lat_from],
                      device(rem(x + 1 + div(j, 8), 4), x, z, core))

    def arrived(slot):
        remote(ts.at[0], x2.at[rows(slot + 3, 1)], t_send.at[0], t_recv.at[slot], partner).wait_recv()

    @pl.when(diagonal)
    def _():
        def pass_on(j, c):
            arrived(19 + j)
            forward(j).start()
            return c

        lax.fori_loop(0, 24, pass_on, 0)

    def arrive(k, c):
        arrived(k)
        return c

    lax.fori_loop(0, 16, arrive, 0)

    def exchange(stage, ref):
        @pl.when(y > 0)
        def _():
            border(stage, 0, ref.at[rows(3, 3)], ref.at[rows(19, 3)]).start()

        @pl.when(y < 3)
        def _():
            border(stage, 1, ref.at[rows(16, 3)], ref.at[rows(0, 3)]).start()

        wait_borders(stage, ref)

    exchange(1, x2)
    sweep(x2, ya, -2, 18)
    sweep(ya, yb, -1, 17)
    sweep(yb, x3, 0, 16)
    exchange(2, x3)
    sweep(x3, ya, -2, 18)
    sweep(ya, yb, -1, 17)

    def give(i):
        return remote(es.at[i], out.at[rows(i, 1), mine], g_send.at[i], g_recv.at[i], partner)

    def last_give(i, c):
        es[i] = one(yb, 8 * other + 2 + i)
        give(i).start()
        return c

    lax.fori_loop(0, 8, last_give, 0)

    def last_keep(i, c):
        out[rows(i, 1), mine] = one(yb, 8 * zh + 2 + i)
        return c

    lax.fori_loop(0, 8, last_keep, 0)

    def finish(i, c):
        remote(es.at[i], out.at[rows(i, 1), theirs], g_send.at[i], g_recv.at[i], partner).wait()
        return c

    lax.fori_loop(0, 8, finish, 0)
    swap_edge.wait_send()
    swap_rest.wait_send()

    @pl.when(edge_chip)
    def _():
        for far in range(2):
            remote(op.at[0], op.at[0], o_send.at[far], o_recv.at[0], partner).wait_send()

    def share_end(k, c):
        remote(op.at[0], op.at[0], o_send.at[1 + k], o_recv.at[0], partner).wait_send()
        return c

    lax.fori_loop(1, 8, share_end, 0)

    @pl.when(y > 0)
    def _():
        remote(op.at[pl.ds(2, 2)], op.at[pl.ds(18, 2)], o_send.at[9], o_recv.at[8], partner).wait_send()
        for stage in range(3):
            border(stage, 0, x1.at[rows(3, 3)], x1.at[rows(19, 3)]).wait_send()

    @pl.when(y < 3)
    def _():
        remote(op.at[pl.ds(16, 2)], op.at[pl.ds(0, 2)], o_send.at[10], o_recv.at[9], partner).wait_send()
        for stage in range(3):
            border(stage, 1, x1.at[rows(3, 3)], x1.at[rows(19, 3)]).wait_send()

    def sent(k, c):
        remote(ts.at[0], x2.at[rows(3, 1)], t_send.at[k], t_recv.at[0], partner).wait_send()
        return c

    lax.fori_loop(1, 16, sent, 0)

    @pl.when(jnp.logical_not(diagonal))
    def _():
        sent(0, 0)

    @pl.when(diagonal)
    def _():
        def passed(j, c):
            forward(j).wait_send()
            return c

        lax.fori_loop(0, 24, passed, 0)


def on_device(covariance, zonal, stencil):
    vmem, dma = pltpu.VMEM, pltpu.SemaphoreType.DMA
    return pl.pallas_call(
        kernel,
        out_shape=jax.ShapeDtypeStruct(covariance.shape, F32),
        in_specs=[pl.BlockSpec(memory_space=pltpu.VMEM)] * 3,
        out_specs=pl.BlockSpec(memory_space=pltpu.VMEM),
        scratch_shapes=[
            vmem((20, N + 8, N), F32),
            vmem((20, N, 3 * N), BF16),
            vmem((20, N, 3 * N), BF16),
            vmem((22 * N, N), F32),
            vmem((46 * N, N), F32),
            vmem((22 * N, N), F32),
            vmem((22 * N, N), F32),
            vmem((22 * N, N), F32),
            vmem((16, N, N), F32),
            vmem((8, N, N), F32),
            dma((2,)), dma((2,)), dma((11,)), dma((10,)), dma((6,)), dma((6,)),
            dma((16,)), dma((43,)), dma((24,)), dma((8,)), dma((8,)),
        ],
        compiler_params=pltpu.CompilerParams(
            collective_id=0, has_side_effects=True, vmem_limit_bytes=60 * 2**20),
        cost_estimate=pl.CostEstimate(flops=6_000_000_000, bytes_accessed=4 * 2**20, transcendentals=0),
        name="propagate",
    )(covariance, zonal, stencil)


def solution(mesh):
    placed = (P("rows", "cols"), P("rows", None, None), P("rows", None, None))
    return jax.shard_map(
        on_device, mesh=mesh, in_specs=placed, out_specs=P("rows", "cols"), check_vma=False
    )
```

```python
import jax
import jax.numpy as jnp
from jax import lax
from jax.experimental import pallas as pl
from jax.experimental.pallas import tpu as pltpu
from jax.sharding import PartitionSpec as P

MESH = pl.DeviceIdType.MESH
N = 128
F32, BF16 = jnp.float32, jnp.bfloat16


def div(a, b):
    return lax.div(a, jnp.int32(b))


def rem(a, b):
    return lax.rem(a, jnp.int32(b))


def device(x, y, z, core):
    return (y * 2 + div(z, 4), x * 8 + rem(z, 4) * 2 + core)


def rows(first, count):
    return pl.ds(pl.multiple_of(first * N, N), count * N)


def kernel(cov, zonal, stencil, out, op, z2, coef, x1, x2, x3, ya, yb, ts, es,
           e_send, e_recv, o_send, o_recv, h_send, h_recv, z_send, z_recv, t_send, t_recv, f_send, g_send, g_recv):
    row, col = lax.axis_index("rows"), lax.axis_index("cols")
    y, zh = div(row, 2), rem(row, 2)
    x, zl, core = div(col, 8), div(rem(col, 8), 2), rem(col, 2)
    z = zh * 4 + zl
    me16 = z * 2 + core
    partner = (row + 1 - 2 * zh, col)
    piece = x * 2 + core
    other = 1 - zh
    edge_chip = (zl == 0) | (zl == 3)
    diagonal = x == y

    def remote(src, dst, send, recv, dev):
        return pltpu.make_async_remote_copy(
            src_ref=src, dst_ref=dst, send_sem=send, recv_sem=recv, device_id=dev, device_id_type=MESH)

    for i in range(8):
        op[2 + 8 * zh + i, 0:N, :] = zonal[i]
        op[2 + 8 * zh + i, N:N + 3, :] = stencil[i]

    @pl.when(y == 0)
    def _():
        op[0:2] = jnp.zeros((2, N + 8, N), F32)
        for ref in (x1, x2, x3):
            ref[0:3 * N, :] = jnp.zeros((3 * N, N), F32)

    @pl.when(y == 3)
    def _():
        op[18:20] = jnp.zeros((2, N + 8, N), F32)
        for ref in (x1, x2, x3):
            ref[19 * N:22 * N, :] = jnp.zeros((3 * N, N), F32)

    barrier = pltpu.get_barrier_semaphore()

    def greet(dev):
        pl.semaphore_signal(barrier, inc=1, device_id=dev, device_id_type=MESH)

    def greet_column(k, c):
        d = rem(me16 + k, 16)
        greet(device(x, y, div(d, 2), rem(d, 2)))
        return c

    lax.fori_loop(1, 16, greet_column, 0)

    def greet_group(k, c):
        q = rem(piece + k, 8)
        greet(device(div(q, 2), y, z, rem(q, 2)))
        return c

    lax.fori_loop(1, 8, greet_group, 0)

    @pl.when(y > 0)
    def _():
        greet(device(x, y - 1, z, core))

    @pl.when(y < 3)
    def _():
        greet(device(x, y + 1, z, core))

    @pl.when(diagonal)
    def _():
        for k in range(1, 4):
            greet(device(x, rem(x + k, 4), z, core))

    @pl.when(jnp.logical_not(diagonal))
    def _():
        greet(device(y, x, z, core))
        greet(device(y, y, z, core))

    writes = 15 + 7 + jnp.where(y > 0, 1, 0) + jnp.where(y < 3, 1, 0) + jnp.where(diagonal, 3, 2)
    pl.semaphore_wait(barrier, writes)

    theirs = pl.ds(pl.multiple_of(other * N, N), N)
    mine = pl.ds(pl.multiple_of(zh * N, N), N)
    swap_edge = remote(cov.at[rows(zh * 5, 3), theirs], x1.at[rows(3 + zh * 13, 3)],
                       e_send.at[0], e_recv.at[0], partner)
    swap_rest = remote(cov.at[rows(other * 3, 5), theirs], x1.at[rows(6 + zh * 5, 5)],
                       e_send.at[1], e_recv.at[1], partner)

    @pl.when(edge_chip)
    def _():
        for far in range(2):
            to = jnp.where(zl == 3, rem(z + 1 + far, 8), rem(z + 7 - far, 8))
            slot = 2 + 8 * zh + piece
            remote(op.at[slot], op.at[slot], o_send.at[far], o_recv.at[piece], device(x, y, to, core)).start()

    swap_edge.start()
    swap_rest.start()

    def border(stage, side, src, dst_first):
        dev = device(x, jnp.where(side == 0, y - 1, y + 1), z, core)
        return remote(src, dst_first, h_send.at[stage * 2 + side], h_recv.at[stage * 2 + side], dev)

    def has(side):
        return jnp.where(side == 0, y > 0, y < 3)

    @pl.when(has(zh))
    def _():
        border(0, zh, cov.at[rows(zh * 5, 3), mine], x1.at[rows(19 - 19 * zh, 3)]).start()

    x1[rows(3 + 8 * zh, 8), :] = cov[:, mine]

    slot = 2 + 8 * other + piece
    remote(op.at[slot], op.at[slot], o_send.at[0], o_recv.at[piece], partner).wait_recv()

    def share(k, c):
        q = rem(piece + k, 8)
        remote(op.at[slot], op.at[slot], o_send.at[1 + k], o_recv.at[piece], device(div(q, 2), y, z, rem(q, 2))).start()
        return c

    lax.fori_loop(1, 8, share, 0)

    def build(l, c):
        z_mat = op[l, 0:N, :]
        hi = z_mat.astype(BF16)
        z2[l, :, 0:N] = hi
        z2[l, :, N:2 * N] = (z_mat - hi.astype(F32)).astype(BF16)
        for part in range(3):
            coef[l, part] = jnp.broadcast_to(op[l, N + part:N + part + 1, :], (N, N)).T
        return c

    lax.fori_loop(2 + 8 * zh, 10 + 8 * zh, build, 0)

    swap_edge.wait_recv()

    @pl.when(has(other))
    def _():
        border(0, other, x1.at[rows(3 + 13 * other, 3)], x1.at[rows(19 - 19 * other, 3)]).start()

    def shared(k, c):
        q = rem(piece + k, 8)
        s = 2 + 8 * other + q
        remote(op.at[s], op.at[s], o_send.at[0], o_recv.at[q], partner).wait_recv()
        return c

    lax.fori_loop(1, 8, shared, 0)

    @pl.when(y > 0)
    def _():
        remote(op.at[pl.ds(2, 2)], op.at[pl.ds(18, 2)], o_send.at[9], o_recv.at[8],
               device(x, y - 1, z, core)).start()

    @pl.when(y < 3)
    def _():
        remote(op.at[pl.ds(16, 2)], op.at[pl.ds(0, 2)], o_send.at[10], o_recv.at[9],
               device(x, y + 1, z, core)).start()

    lax.fori_loop(2 + 8 * other, 10 + 8 * other, build, 0)

    @pl.when(y < 3)
    def _():
        remote(op.at[pl.ds(18, 2)], op.at[pl.ds(18, 2)], o_send.at[0], o_recv.at[8], partner).wait_recv()

    @pl.when(y > 0)
    def _():
        remote(op.at[pl.ds(0, 2)], op.at[pl.ds(0, 2)], o_send.at[0], o_recv.at[9], partner).wait_recv()

    lax.fori_loop(0, 2, build, 0)
    lax.fori_loop(18, 20, build, 0)

    def one(src, i):
        v = src[rows(i, 3), :]
        v = coef[i, 0] * v[N:2 * N] + coef[i, 1] * v[2 * N:] + coef[i, 2] * v[0:N]
        hi = v.astype(BF16)
        lo = (v - hi.astype(F32)).astype(BF16)
        right = jnp.concatenate(
            [jnp.concatenate([hi, hi], axis=0), jnp.concatenate([lo, jnp.zeros_like(lo)], axis=0)], axis=1)
        both = jnp.dot(z2[i], right, preferred_element_type=F32)
        return both[:, 0:N] + both[:, N:]

    def sweep(src, dst, first, last, unroll):
        def body(i, c):
            dst[rows(i + 1, 1), :] = one(src, i)
            return c

        lax.fori_loop(first + 2, last + 2, body, 0, unroll=unroll)

    def wait_borders(stage, ref):
        @pl.when(y < 3)
        def _():
            border(stage, 0, ref.at[rows(19, 3)], ref.at[rows(19, 3)]).wait_recv()

        @pl.when(y > 0)
        def _():
            border(stage, 1, ref.at[rows(0, 3)], ref.at[rows(0, 3)]).wait_recv()

    swap_rest.wait_recv()
    wait_borders(0, x1)
    sweep(x1, ya, -2, 18, 5)
    sweep(ya, yb, -1, 17, 6)

    def turn(lat, c):
        ts[lat] = one(yb, lat + 2).T
        return c

    lax.fori_loop(0, 16, turn, 0, unroll=8)

    def order(i):
        return jnp.where(rem(i, 2) == 1, div(i + 1, 2), jnp.where(i == 0, 0, 16 - div(i, 2)))

    def block_of(d):
        zt = div(d, 2)
        return 8 * div(rem(zt, 4), 2) + 4 * rem(zt, 2) + 2 * rem(d, 2) + div(zt, 4)

    def place(s):
        return 3 + rem(div(s, 2), 4) * 4 + rem(s, 2) * 2 + div(s, 8)

    def landing(s):
        return rows(jnp.where(diagonal, place(s), 46 + s), 1)

    self_copy = pltpu.make_async_copy(ts.at[block_of(me16)], x2.at[landing(me16)], z_recv.at[me16])
    self_copy.start()

    def column_send(i, c):
        d = rem(me16 + order(i), 16)
        remote(ts.at[block_of(d)], x2.at[landing(me16)], z_send.at[i], z_recv.at[me16],
               device(x, y, div(d, 2), rem(d, 2))).start()
        return c

    lax.fori_loop(1, 16, column_send, 0)

    def source(i):
        return rem(me16 - order(i) + 16, 16)

    def column_wait(i, c):
        s = source(i)
        remote(ts.at[0], x2.at[landing(s)], z_send.at[0], z_recv.at[s], partner).wait_recv()
        return c

    def onward(i):
        s = source(i)
        relay = rem(i, 2) == 1
        slot = jnp.where(relay, 22 + rem(y + 3 - x, 4) * 8 + div(i, 2), place(s))
        sem = jnp.where(relay, 16 + rem(y + 3 - x, 4) * 8 + div(i, 2), s)
        return remote(x2.at[landing(s)], x2.at[rows(slot, 1)], t_send.at[i], t_recv.at[sem],
                      device(jnp.where(relay, x, y), x, z, core))

    def forward(j):
        m, o = div(j, 3), rem(j, 3)
        s = source(2 * m + 1)
        return remote(x2.at[rows(22 + o * 8 + m, 1)], x2.at[rows(place(s), 1)], f_send.at[j], t_recv.at[s],
                      device(rem(x + 1 + o, 4), x, z, core))

    @pl.when(jnp.logical_not(diagonal))
    def _():
        def go(i, c):
            column_wait(i, 0)
            onward(i).start()
            return c

        lax.fori_loop(0, 16, go, 0)

        def arrive(s, c):
            remote(ts.at[0], x2.at[rows(place(s), 1)], z_send.at[0], t_recv.at[s], partner).wait_recv()
            return c

        lax.fori_loop(0, 16, arrive, 0)

    @pl.when(diagonal)
    def _():
        def pass_on(j, c):
            slot = rem(j, 3) * 8 + div(j, 3)
            remote(ts.at[0], x2.at[rows(22 + slot, 1)], z_send.at[0], t_recv.at[16 + slot], partner).wait_recv()
            forward(j).start()
            return c

        lax.fori_loop(0, 24, pass_on, 0)
        lax.fori_loop(0, 16, column_wait, 0)

    def exchange(stage, ref):
        @pl.when(y > 0)
        def _():
            border(stage, 0, ref.at[rows(3, 3)], ref.at[rows(19, 3)]).start()

        @pl.when(y < 3)
        def _():
            border(stage, 1, ref.at[rows(16, 3)], ref.at[rows(0, 3)]).start()

        wait_borders(stage, ref)

    exchange(1, x2)
    sweep(x2, ya, -2, 18, 5)
    sweep(ya, yb, -1, 17, 6)
    sweep(yb, x3, 0, 16, 8)
    exchange(2, x3)
    sweep(x3, ya, -2, 18, 5)
    sweep(ya, yb, -1, 17, 6)

    def give(i):
        return remote(es.at[i], out.at[rows(i, 1), mine], g_send.at[i], g_recv.at[i], partner)

    def last_give(i, c):
        es[i] = one(yb, 8 * other + 2 + i)
        give(i).start()
        return c

    lax.fori_loop(0, 8, last_give, 0, unroll=4)

    def last_keep(i, c):
        out[rows(i, 1), mine] = one(yb, 8 * zh + 2 + i)
        return c

    lax.fori_loop(0, 8, last_keep, 0, unroll=4)

    def finish(i, c):
        remote(es.at[i], out.at[rows(i, 1), theirs], g_send.at[i], g_recv.at[i], partner).wait()
        return c

    lax.fori_loop(0, 8, finish, 0)
    swap_edge.wait_send()
    swap_rest.wait_send()

    @pl.when(edge_chip)
    def _():
        for far in range(2):
            remote(op.at[0], op.at[0], o_send.at[far], o_recv.at[0], partner).wait_send()

    def share_end(k, c):
        remote(op.at[0], op.at[0], o_send.at[1 + k], o_recv.at[0], partner).wait_send()
        return c

    lax.fori_loop(1, 8, share_end, 0)

    @pl.when(y > 0)
    def _():
        remote(op.at[pl.ds(2, 2)], op.at[pl.ds(18, 2)], o_send.at[9], o_recv.at[8], partner).wait_send()
        for stage in range(3):
            border(stage, 0, x1.at[rows(3, 3)], x1.at[rows(19, 3)]).wait_send()

    @pl.when(y < 3)
    def _():
        remote(op.at[pl.ds(16, 2)], op.at[pl.ds(0, 2)], o_send.at[10], o_recv.at[9], partner).wait_send()
        for stage in range(3):
            border(stage, 1, x1.at[rows(3, 3)], x1.at[rows(19, 3)]).wait_send()

    def sent(i, c):
        remote(ts.at[0], x2.at[rows(3, 1)], z_send.at[i], z_recv.at[0], partner).wait_send()
        return c

    lax.fori_loop(1, 16, sent, 0)

    @pl.when(jnp.logical_not(diagonal))
    def _():
        def gone(i, c):
            onward(i).wait_send()
            return c

        lax.fori_loop(0, 16, gone, 0)

    @pl.when(diagonal)
    def _():
        def passed(j, c):
            forward(j).wait_send()
            return c

        lax.fori_loop(0, 24, passed, 0)


def on_device(covariance, zonal, stencil):
    vmem, dma = pltpu.VMEM, pltpu.SemaphoreType.DMA
    return pl.pallas_call(
        kernel,
        out_shape=jax.ShapeDtypeStruct(covariance.shape, F32),
        in_specs=[pl.BlockSpec(memory_space=pltpu.VMEM)] * 3,
        out_specs=pl.BlockSpec(memory_space=pltpu.VMEM),
        scratch_shapes=[
            vmem((20, N + 8, N), F32),
            vmem((20, N, 2 * N), BF16),
            vmem((20, 3, N, N), F32),
            vmem((22 * N, N), F32),
            vmem((62 * N, N), F32),
            vmem((22 * N, N), F32),
            vmem((22 * N, N), F32),
            vmem((22 * N, N), F32),
            vmem((16, N, N), F32),
            vmem((8, N, N), F32),
            dma((2,)), dma((2,)), dma((11,)), dma((10,)), dma((6,)), dma((6,)),
            dma((16,)), dma((16,)), dma((16,)), dma((40,)), dma((24,)), dma((8,)), dma((8,)),
        ],
        compiler_params=pltpu.CompilerParams(
            collective_id=0, has_side_effects=True, vmem_limit_bytes=60 * 2**20),
        cost_estimate=pl.CostEstimate(flops=2_000_000_000, bytes_accessed=4 * 2**20, transcendentals=0),
        name="propagate",
    )(covariance, zonal, stencil)


def solution(mesh):
    placed = (P("rows", "cols"), P("rows", None, None), P("rows", None, None))
    return jax.shard_map(
        on_device, mesh=mesh, in_specs=placed, out_specs=P("rows", "cols"), check_vma=False
    )
```

```python
import jax
import jax.numpy as jnp
from jax import lax
from jax.experimental import pallas as pl
from jax.experimental.pallas import tpu as pltpu
from jax.sharding import PartitionSpec as P

MESH = pl.DeviceIdType.MESH
N = 128
F32, BF16 = jnp.float32, jnp.bfloat16


def div(a, b):
    return lax.div(a, jnp.int32(b))


def rem(a, b):
    return lax.rem(a, jnp.int32(b))


def device(x, y, z, core):
    return (y * 2 + div(z, 4), x * 8 + rem(z, 4) * 2 + core)


def rows(first, count):
    return pl.ds(pl.multiple_of(first * N, N), count * N)


def kernel(cov, zonal, stencil, out, op, z2, coef, x1, x2, x3, ya, yb, ts, es,
           e_send, e_recv, o_send, o_recv, h_send, h_recv, z_send, z_recv, t_send, t_recv, f_send, g_send, g_recv):
    row, col = lax.axis_index("rows"), lax.axis_index("cols")
    y, zh = div(row, 2), rem(row, 2)
    x, zl, core = div(col, 8), div(rem(col, 8), 2), rem(col, 2)
    z = zh * 4 + zl
    me16 = z * 2 + core
    partner = (row + 1 - 2 * zh, col)
    piece = x * 2 + core
    other = 1 - zh
    diagonal = x == y

    def remote(src, dst, send, recv, dev):
        return pltpu.make_async_remote_copy(
            src_ref=src, dst_ref=dst, send_sem=send, recv_sem=recv, device_id=dev, device_id_type=MESH)

    for i in range(8):
        op[2 + 8 * zh + i, 0:N, :] = zonal[i]
        op[2 + 8 * zh + i, N:N + 3, :] = stencil[i]

    @pl.when(y == 0)
    def _():
        op[0:2] = jnp.zeros((2, N + 8, N), F32)
        for ref in (x1, x2, x3):
            ref[0:3 * N, :] = jnp.zeros((3 * N, N), F32)

    @pl.when(y == 3)
    def _():
        op[18:20] = jnp.zeros((2, N + 8, N), F32)
        for ref in (x1, x2, x3):
            ref[19 * N:22 * N, :] = jnp.zeros((3 * N, N), F32)

    barrier = pltpu.get_barrier_semaphore()

    def greet(dev):
        pl.semaphore_signal(barrier, inc=1, device_id=dev, device_id_type=MESH)

    def greet_column(k, c):
        d = rem(me16 + k, 16)
        greet(device(x, y, div(d, 2), rem(d, 2)))
        return c

    lax.fori_loop(1, 16, greet_column, 0)

    def greet_group(k, c):
        q = rem(piece + k, 8)
        greet(device(div(q, 2), y, z, rem(q, 2)))
        return c

    lax.fori_loop(1, 8, greet_group, 0)

    @pl.when(y > 0)
    def _():
        greet(device(x, y - 1, z, core))

    @pl.when(y < 3)
    def _():
        greet(device(x, y + 1, z, core))

    @pl.when(diagonal)
    def _():
        for k in range(1, 4):
            greet(device(x, rem(x + k, 4), z, core))

    @pl.when(jnp.logical_not(diagonal))
    def _():
        greet(device(y, x, z, core))
        greet(device(y, y, z, core))

    writes = 15 + 7 + jnp.where(y > 0, 1, 0) + jnp.where(y < 3, 1, 0) + jnp.where(diagonal, 3, 2)
    pl.semaphore_wait(barrier, writes)

    theirs = pl.ds(pl.multiple_of(other * N, N), N)
    mine = pl.ds(pl.multiple_of(zh * N, N), N)
    swap_edge = remote(cov.at[rows(zh * 5, 3), theirs], x1.at[rows(3 + zh * 13, 3)],
                       e_send.at[0], e_recv.at[0], partner)
    swap_rest = remote(cov.at[rows(other * 3, 5), theirs], x1.at[rows(6 + zh * 5, 5)],
                       e_send.at[1], e_recv.at[1], partner)

    kept = 2 + 8 * zh + piece
    gotten = 2 + 8 * other + piece
    remote(op.at[kept], op.at[kept], o_send.at[0], o_recv.at[piece], partner).start()
    swap_edge.start()
    swap_rest.start()

    def border(stage, side, src, dst_first):
        dev = device(x, jnp.where(side == 0, y - 1, y + 1), z, core)
        return remote(src, dst_first, h_send.at[stage * 2 + side], h_recv.at[stage * 2 + side], dev)

    def has(side):
        return jnp.where(side == 0, y > 0, y < 3)

    @pl.when(has(zh))
    def _():
        border(0, zh, cov.at[rows(zh * 5, 3), mine], x1.at[rows(19 - 19 * zh, 3)]).start()

    x1[rows(3 + 8 * zh, 8), :] = cov[:, mine]

    def build(l, c):
        z_mat = op[l, 0:N, :]
        hi = z_mat.astype(BF16)
        z2[l, :, 0:N] = hi
        z2[l, :, N:2 * N] = (z_mat - hi.astype(F32)).astype(BF16)
        for part in range(3):
            coef[l, part] = jnp.broadcast_to(op[l, N + part:N + part + 1, :], (N, N)).T
        return c

    lax.fori_loop(2 + 8 * zh, 10 + 8 * zh, build, 0)

    remote(op.at[gotten], op.at[gotten], o_send.at[0], o_recv.at[piece], partner).wait_recv()

    def share(k, c):
        q = rem(piece + k, 8)
        remote(op.at[gotten], op.at[gotten], o_send.at[k], o_recv.at[piece], device(div(q, 2), y, z, rem(q, 2))).start()
        return c

    lax.fori_loop(1, 8, share, 0)

    def shared(k, c):
        q = rem(piece + k, 8)
        s = 2 + 8 * other + q
        remote(op.at[s], op.at[s], o_send.at[0], o_recv.at[q], partner).wait_recv()
        return c

    lax.fori_loop(1, 8, shared, 0)

    @pl.when(y > 0)
    def _():
        remote(op.at[pl.ds(2, 2)], op.at[pl.ds(18, 2)], o_send.at[9], o_recv.at[8],
               device(x, y - 1, z, core)).start()

    @pl.when(y < 3)
    def _():
        remote(op.at[pl.ds(16, 2)], op.at[pl.ds(0, 2)], o_send.at[10], o_recv.at[9],
               device(x, y + 1, z, core)).start()

    swap_edge.wait_recv()

    @pl.when(has(other))
    def _():
        border(0, other, x1.at[rows(3 + 13 * other, 3)], x1.at[rows(19 - 19 * other, 3)]).start()

    lax.fori_loop(2 + 8 * other, 10 + 8 * other, build, 0)

    @pl.when(y < 3)
    def _():
        remote(op.at[pl.ds(18, 2)], op.at[pl.ds(18, 2)], o_send.at[0], o_recv.at[8], partner).wait_recv()

    @pl.when(y > 0)
    def _():
        remote(op.at[pl.ds(0, 2)], op.at[pl.ds(0, 2)], o_send.at[0], o_recv.at[9], partner).wait_recv()

    lax.fori_loop(0, 2, build, 0)
    lax.fori_loop(18, 20, build, 0)

    def one(src, i):
        v = src[rows(i, 3), :]
        v = coef[i, 0] * v[N:2 * N] + coef[i, 1] * v[2 * N:] + coef[i, 2] * v[0:N]
        hi = v.astype(BF16)
        lo = (v - hi.astype(F32)).astype(BF16)
        right = jnp.concatenate(
            [jnp.concatenate([hi, hi], axis=0), jnp.concatenate([lo, jnp.zeros_like(lo)], axis=0)], axis=1)
        both = jnp.dot(z2[i], right, preferred_element_type=F32)
        return both[:, 0:N] + both[:, N:]

    def sweep(src, dst, first, last, unroll):
        def body(i, c):
            dst[rows(i + 1, 1), :] = one(src, i)
            return c

        lax.fori_loop(first + 2, last + 2, body, 0, unroll=unroll)

    def wait_borders(stage, ref):
        @pl.when(y < 3)
        def _():
            border(stage, 0, ref.at[rows(19, 3)], ref.at[rows(19, 3)]).wait_recv()

        @pl.when(y > 0)
        def _():
            border(stage, 1, ref.at[rows(0, 3)], ref.at[rows(0, 3)]).wait_recv()

    swap_rest.wait_recv()
    wait_borders(0, x1)
    sweep(x1, ya, -2, 18, 5)
    sweep(ya, yb, -1, 17, 6)

    def turn(lat, c):
        ts[lat] = one(yb, lat + 2).T
        return c

    lax.fori_loop(0, 16, turn, 0, unroll=8)

    def order(i):
        return jnp.where(rem(i, 2) == 1, div(i + 1, 2), jnp.where(i == 0, 0, 16 - div(i, 2)))

    def block_of(d):
        zt = div(d, 2)
        return 8 * div(rem(zt, 4), 2) + 4 * rem(zt, 2) + 2 * rem(d, 2) + div(zt, 4)

    def place(s):
        return 3 + rem(div(s, 2), 4) * 4 + rem(s, 2) * 2 + div(s, 8)

    def landing(s):
        return rows(jnp.where(diagonal, place(s), 46 + s), 1)

    self_copy = pltpu.make_async_copy(ts.at[block_of(me16)], x2.at[landing(me16)], z_recv.at[me16])
    self_copy.start()

    def column_send(i, c):
        d = rem(me16 + order(i), 16)
        remote(ts.at[block_of(d)], x2.at[landing(me16)], z_send.at[i], z_recv.at[me16],
               device(x, y, div(d, 2), rem(d, 2))).start()
        return c

    lax.fori_loop(1, 16, column_send, 0)

    def source(i):
        return rem(me16 - order(i) + 16, 16)

    def column_wait(i, c):
        s = source(i)
        remote(ts.at[0], x2.at[landing(s)], z_send.at[0], z_recv.at[s], partner).wait_recv()
        return c

    def onward(i):
        s = source(i)
        relay = rem(i, 2) == 1
        slot = jnp.where(relay, 22 + rem(y + 3 - x, 4) * 8 + div(i, 2), place(s))
        sem = jnp.where(relay, 16 + rem(y + 3 - x, 4) * 8 + div(i, 2), s)
        return remote(x2.at[landing(s)], x2.at[rows(slot, 1)], t_send.at[i], t_recv.at[sem],
                      device(jnp.where(relay, x, y), x, z, core))

    def forward(j):
        m, o = div(j, 3), rem(j, 3)
        s = source(2 * m + 1)
        return remote(x2.at[rows(22 + o * 8 + m, 1)], x2.at[rows(place(s), 1)], f_send.at[j], t_recv.at[s],
                      device(rem(x + 1 + o, 4), x, z, core))

    @pl.when(jnp.logical_not(diagonal))
    def _():
        def go(i, c):
            column_wait(i, 0)
            onward(i).start()
            return c

        lax.fori_loop(0, 16, go, 0)

        def arrive(s, c):
            remote(ts.at[0], x2.at[rows(place(s), 1)], z_send.at[0], t_recv.at[s], partner).wait_recv()
            return c

        lax.fori_loop(0, 16, arrive, 0)

    @pl.when(diagonal)
    def _():
        def pass_on(j, c):
            slot = rem(j, 3) * 8 + div(j, 3)
            remote(ts.at[0], x2.at[rows(22 + slot, 1)], z_send.at[0], t_recv.at[16 + slot], partner).wait_recv()
            forward(j).start()
            return c

        lax.fori_loop(0, 24, pass_on, 0)
        lax.fori_loop(0, 16, column_wait, 0)

    def exchange(stage, ref):
        @pl.when(y > 0)
        def _():
            border(stage, 0, ref.at[rows(3, 3)], ref.at[rows(19, 3)]).start()

        @pl.when(y < 3)
        def _():
            border(stage, 1, ref.at[rows(16, 3)], ref.at[rows(0, 3)]).start()

    def edges(src, dst, first):
        def body(k, c):
            for i in (first + 2 + k, 15 - first + k):
                dst[rows(i + 1, 1), :] = one(src, i)
            return c

        lax.fori_loop(0, 3, body, 0, unroll=3)

    exchange(1, x2)
    sweep(x2, ya, 1, 15, 7)
    sweep(ya, yb, 2, 14, 6)
    sweep(yb, x3, 3, 13, 5)
    wait_borders(1, x2)
    edges(x2, ya, -2)
    edges(ya, yb, -1)
    edges(yb, x3, 0)
    exchange(2, x3)
    sweep(x3, ya, 1, 15, 7)
    sweep(ya, yb, 2, 14, 6)

    def give(i):
        return remote(es.at[i], out.at[rows(i, 1), mine], g_send.at[i], g_recv.at[i], partner)

    def last_give(i, c):
        es[i] = one(yb, 8 * other + 2 + i)
        give(i).start()
        return c

    lax.fori_loop(0, 5, lambda k, c: last_give(3 * zh + k, c), 0, unroll=5)
    wait_borders(2, x3)
    edges(x3, ya, -2)
    edges(ya, yb, -1)
    lax.fori_loop(0, 3, lambda k, c: last_give(5 * other + k, c), 0, unroll=3)

    def last_keep(i, c):
        out[rows(i, 1), mine] = one(yb, 8 * zh + 2 + i)
        return c

    lax.fori_loop(0, 8, last_keep, 0, unroll=4)

    def finish(i, c):
        remote(es.at[i], out.at[rows(i, 1), theirs], g_send.at[i], g_recv.at[i], partner).wait()
        return c

    lax.fori_loop(0, 8, finish, 0)
    swap_edge.wait_send()
    swap_rest.wait_send()

    remote(op.at[0], op.at[0], o_send.at[0], o_recv.at[0], partner).wait_send()

    def share_end(k, c):
        remote(op.at[0], op.at[0], o_send.at[k], o_recv.at[0], partner).wait_send()
        return c

    lax.fori_loop(1, 8, share_end, 0)

    @pl.when(y > 0)
    def _():
        remote(op.at[pl.ds(2, 2)], op.at[pl.ds(18, 2)], o_send.at[9], o_recv.at[8], partner).wait_send()
        for stage in range(3):
            border(stage, 0, x1.at[rows(3, 3)], x1.at[rows(19, 3)]).wait_send()

    @pl.when(y < 3)
    def _():
        remote(op.at[pl.ds(16, 2)], op.at[pl.ds(0, 2)], o_send.at[10], o_recv.at[9], partner).wait_send()
        for stage in range(3):
            border(stage, 1, x1.at[rows(3, 3)], x1.at[rows(19, 3)]).wait_send()

    def sent(i, c):
        remote(ts.at[0], x2.at[rows(3, 1)], z_send.at[i], z_recv.at[0], partner).wait_send()
        return c

    lax.fori_loop(1, 16, sent, 0)

    @pl.when(jnp.logical_not(diagonal))
    def _():
        def gone(i, c):
            onward(i).wait_send()
            return c

        lax.fori_loop(0, 16, gone, 0)

    @pl.when(diagonal)
    def _():
        def passed(j, c):
            forward(j).wait_send()
            return c

        lax.fori_loop(0, 24, passed, 0)


def on_device(covariance, zonal, stencil):
    vmem, dma = pltpu.VMEM, pltpu.SemaphoreType.DMA
    return pl.pallas_call(
        kernel,
        out_shape=jax.ShapeDtypeStruct(covariance.shape, F32),
        in_specs=[pl.BlockSpec(memory_space=pltpu.VMEM)] * 3,
        out_specs=pl.BlockSpec(memory_space=pltpu.VMEM),
        scratch_shapes=[
            vmem((20, N + 8, N), F32),
            vmem((20, N, 2 * N), BF16),
            vmem((20, 3, N, N), F32),
            vmem((22 * N, N), F32),
            vmem((62 * N, N), F32),
            vmem((22 * N, N), F32),
            vmem((22 * N, N), F32),
            vmem((22 * N, N), F32),
            vmem((16, N, N), F32),
            vmem((8, N, N), F32),
            dma((2,)), dma((2,)), dma((11,)), dma((10,)), dma((6,)), dma((6,)),
            dma((16,)), dma((16,)), dma((16,)), dma((40,)), dma((24,)), dma((8,)), dma((8,)),
        ],
        compiler_params=pltpu.CompilerParams(
            collective_id=0, has_side_effects=True, vmem_limit_bytes=60 * 2**20),
        cost_estimate=pl.CostEstimate(flops=2_000_000_000, bytes_accessed=4 * 2**20, transcendentals=0),
        name="propagate",
    )(covariance, zonal, stencil)


def solution(mesh):
    placed = (P("rows", "cols"), P("rows", None, None), P("rows", None, None))
    return jax.shard_map(
        on_device, mesh=mesh, in_specs=placed, out_specs=P("rows", "cols"), check_vma=False
    )
```

```python
import jax
import jax.numpy as jnp
from jax import lax
from jax.experimental import pallas as pl
from jax.experimental.pallas import tpu as pltpu
from jax.sharding import PartitionSpec as P

MESH = pl.DeviceIdType.MESH
N = 128
F32, BF16 = jnp.float32, jnp.bfloat16


def div(a, b):
    return lax.div(a, jnp.int32(b))


def rem(a, b):
    return lax.rem(a, jnp.int32(b))


def device(x, y, z, core):
    return (y * 2 + div(z, 4), x * 8 + rem(z, 4) * 2 + core)


def rows(first, count):
    return pl.ds(pl.multiple_of(first * N, N), count * N)


def kernel(cov, zonal, stencil, out, op, z2, coef, x1, x2, x3, ya, yb, s4, s5, ts, es,
           e_send, e_recv, o_send, o_recv, h_send, h_recv, z_send, z_recv, t_send, t_recv, f_send, g_send, g_recv):
    row, col = lax.axis_index("rows"), lax.axis_index("cols")
    y, zh = div(row, 2), rem(row, 2)
    x, zl, core = div(col, 8), div(rem(col, 8), 2), rem(col, 2)
    z = zh * 4 + zl
    me16 = z * 2 + core
    partner = (row + 1 - 2 * zh, col)
    piece = x * 2 + core
    other = 1 - zh
    diagonal = x == y

    def remote(src, dst, send, recv, dev):
        return pltpu.make_async_remote_copy(
            src_ref=src, dst_ref=dst, send_sem=send, recv_sem=recv, device_id=dev, device_id_type=MESH)

    op[pl.ds(2 + 8 * zh, 8), 0:N, :] = zonal[...]
    for i in range(8):
        for part in range(3):
            op[2 + 8 * zh + i, N + part:N + part + 1, :] = stencil[part, i:i + 1, :]

    @pl.when(y == 0)
    def _():
        op[0:2] = jnp.zeros((2, N + 8, N), F32)
        for ref in (x1, x2, x3):
            ref[0:3 * N, :] = jnp.zeros((3 * N, N), F32)

    @pl.when(y == 3)
    def _():
        op[18:20] = jnp.zeros((2, N + 8, N), F32)
        for ref in (x1, x2, x3):
            ref[19 * N:22 * N, :] = jnp.zeros((3 * N, N), F32)

    barrier = pltpu.get_barrier_semaphore()

    def greet(dev):
        pl.semaphore_signal(barrier, inc=1, device_id=dev, device_id_type=MESH)

    def greet_column(k, c):
        d = rem(me16 + k, 16)
        greet(device(x, y, div(d, 2), rem(d, 2)))
        return c

    lax.fori_loop(1, 16, greet_column, 0)

    def greet_group(k, c):
        q = rem(piece + k, 8)
        greet(device(div(q, 2), y, z, rem(q, 2)))
        return c

    lax.fori_loop(1, 8, greet_group, 0)

    @pl.when(y > 0)
    def _():
        greet(device(x, y - 1, z, core))

    @pl.when(y < 3)
    def _():
        greet(device(x, y + 1, z, core))

    @pl.when(diagonal)
    def _():
        for k in range(1, 4):
            greet(device(x, rem(x + k, 4), z, core))

    @pl.when(jnp.logical_not(diagonal))
    def _():
        greet(device(y, x, z, core))
        greet(device(y, y, z, core))

    writes = 15 + 7 + jnp.where(y > 0, 1, 0) + jnp.where(y < 3, 1, 0) + jnp.where(diagonal, 3, 2)
    pl.semaphore_wait(barrier, writes)

    theirs = pl.ds(pl.multiple_of(other * N, N), N)
    mine = pl.ds(pl.multiple_of(zh * N, N), N)
    swap_edge = remote(cov.at[rows(zh * 5, 3), theirs], x1.at[rows(3 + zh * 13, 3)],
                       e_send.at[0], e_recv.at[0], partner)
    swap_rest = remote(cov.at[rows(other * 3, 5), theirs], x1.at[rows(6 + zh * 5, 5)],
                       e_send.at[1], e_recv.at[1], partner)

    kept = 2 + 8 * zh + piece
    gotten = 2 + 8 * other + piece
    remote(op.at[kept], op.at[kept], o_send.at[0], o_recv.at[piece], partner).start()
    swap_edge.start()
    swap_rest.start()

    def border(stage, side, src, dst_first):
        dev = device(x, jnp.where(side == 0, y - 1, y + 1), z, core)
        return remote(src, dst_first, h_send.at[stage * 2 + side], h_recv.at[stage * 2 + side], dev)

    def has(side):
        return jnp.where(side == 0, y > 0, y < 3)

    @pl.when(has(zh))
    def _():
        border(0, zh, cov.at[rows(zh * 5, 3), mine], x1.at[rows(19 - 19 * zh, 3)]).start()

    x1[rows(3 + 8 * zh, 8), :] = cov[:, mine]

    def build(l, c):
        z_mat = op[l, 0:N, :]
        hi = z_mat.astype(BF16)
        z2[l, :, 0:N] = hi
        z2[l, :, N:2 * N] = (z_mat - hi.astype(F32)).astype(BF16)
        for part in range(3):
            coef[l, part] = jnp.broadcast_to(op[l, N + part:N + part + 1, :], (N, N)).T
        return c

    lax.fori_loop(2 + 8 * zh, 10 + 8 * zh, build, 0)

    remote(op.at[gotten], op.at[gotten], o_send.at[0], o_recv.at[piece], partner).wait_recv()

    def share(k, c):
        q = rem(piece + k, 8)
        remote(op.at[gotten], op.at[gotten], o_send.at[k], o_recv.at[piece], device(div(q, 2), y, z, rem(q, 2))).start()
        return c

    lax.fori_loop(1, 8, share, 0)

    def shared(k, c):
        q = rem(piece + k, 8)
        s = 2 + 8 * other + q
        remote(op.at[s], op.at[s], o_send.at[0], o_recv.at[q], partner).wait_recv()
        return c

    lax.fori_loop(1, 8, shared, 0)

    @pl.when(y > 0)
    def _():
        remote(op.at[pl.ds(2, 2)], op.at[pl.ds(18, 2)], o_send.at[9], o_recv.at[8],
               device(x, y - 1, z, core)).start()

    @pl.when(y < 3)
    def _():
        remote(op.at[pl.ds(16, 2)], op.at[pl.ds(0, 2)], o_send.at[10], o_recv.at[9],
               device(x, y + 1, z, core)).start()

    swap_edge.wait_recv()

    @pl.when(has(other))
    def _():
        border(0, other, x1.at[rows(3 + 13 * other, 3)], x1.at[rows(19 - 19 * other, 3)]).start()

    lax.fori_loop(2 + 8 * other, 10 + 8 * other, build, 0)

    @pl.when(y < 3)
    def _():
        remote(op.at[pl.ds(18, 2)], op.at[pl.ds(18, 2)], o_send.at[0], o_recv.at[8], partner).wait_recv()

    @pl.when(y > 0)
    def _():
        remote(op.at[pl.ds(0, 2)], op.at[pl.ds(0, 2)], o_send.at[0], o_recv.at[9], partner).wait_recv()

    lax.fori_loop(0, 2, build, 0)
    lax.fori_loop(18, 20, build, 0)

    def one(src, i):
        v = src[rows(i, 3), :]
        v = coef[i, 0] * v[N:2 * N] + coef[i, 1] * v[2 * N:] + coef[i, 2] * v[0:N]
        hi = v.astype(BF16)
        lo = (v - hi.astype(F32)).astype(BF16)
        right = jnp.concatenate(
            [jnp.concatenate([hi, hi], axis=0), jnp.concatenate([lo, jnp.zeros_like(lo)], axis=0)], axis=1)
        both = jnp.dot(z2[i], right, preferred_element_type=F32)
        return both[:, 0:N] + both[:, N:]

    def sweep(src, dst, first, last, unroll):
        def body(i, c):
            dst[rows(i + 1, 1), :] = one(src, i)
            return c

        lax.fori_loop(first + 2, last + 2, body, 0, unroll=unroll)

    def wait_borders(stage, ref):
        @pl.when(y < 3)
        def _():
            border(stage, 0, ref.at[rows(19, 3)], ref.at[rows(19, 3)]).wait_recv()

        @pl.when(y > 0)
        def _():
            border(stage, 1, ref.at[rows(0, 3)], ref.at[rows(0, 3)]).wait_recv()

    swap_rest.wait_recv()
    wait_borders(0, x1)
    sweep(x1, ya, -2, 18, 5)
    sweep(ya, yb, -1, 17, 6)

    def turn(lat, c):
        ts[lat] = one(yb, lat + 2).T
        return c

    lax.fori_loop(0, 16, turn, 0, unroll=8)

    def order(i):
        return jnp.where(rem(i, 2) == 1, div(i + 1, 2), jnp.where(i == 0, 0, 16 - div(i, 2)))

    def block_of(d):
        zt = div(d, 2)
        return 8 * div(rem(zt, 4), 2) + 4 * rem(zt, 2) + 2 * rem(d, 2) + div(zt, 4)

    def place(s):
        return 3 + rem(div(s, 2), 4) * 4 + rem(s, 2) * 2 + div(s, 8)

    def landing(s):
        return rows(jnp.where(diagonal, place(s), 46 + s), 1)

    self_copy = pltpu.make_async_copy(ts.at[block_of(me16)], x2.at[landing(me16)], z_recv.at[me16])
    self_copy.start()

    def column_send(i, c):
        d = rem(me16 + order(i), 16)
        remote(ts.at[block_of(d)], x2.at[landing(me16)], z_send.at[i], z_recv.at[me16],
               device(x, y, div(d, 2), rem(d, 2))).start()
        return c

    lax.fori_loop(1, 16, column_send, 0)

    def source(i):
        return rem(me16 - order(i) + 16, 16)

    def column_wait(i, c):
        s = source(i)
        remote(ts.at[0], x2.at[landing(s)], z_send.at[0], z_recv.at[s], partner).wait_recv()
        return c

    def onward(i):
        s = source(i)
        relay = rem(i, 2) == 0
        slot = jnp.where(relay, 22 + rem(y + 3 - x, 4) * 8 + div(i, 2), place(s))
        sem = jnp.where(relay, 16 + rem(y + 3 - x, 4) * 8 + div(i, 2), s)
        return remote(x2.at[landing(s)], x2.at[rows(slot, 1)], t_send.at[i], t_recv.at[sem],
                      device(jnp.where(relay, x, y), x, z, core))

    def forward(j):
        m, o = div(j, 3), rem(j, 3)
        s = source(2 * m)
        return remote(x2.at[rows(22 + o * 8 + m, 1)], x2.at[rows(place(s), 1)], f_send.at[j], t_recv.at[s],
                      device(rem(x + 1 + o, 4), x, z, core))

    @pl.when(jnp.logical_not(diagonal))
    def _():
        def go(i, c):
            column_wait(i, 0)
            onward(i).start()
            return c

        lax.fori_loop(0, 16, go, 0)

        def arrive(s, c):
            remote(ts.at[0], x2.at[rows(place(s), 1)], z_send.at[0], t_recv.at[s], partner).wait_recv()
            return c

        lax.fori_loop(0, 16, arrive, 0)

    @pl.when(diagonal)
    def _():
        def pass_on(j, c):
            slot = rem(j, 3) * 8 + div(j, 3)
            remote(ts.at[0], x2.at[rows(22 + slot, 1)], z_send.at[0], t_recv.at[16 + slot], partner).wait_recv()
            forward(j).start()
            return c

        lax.fori_loop(0, 24, pass_on, 0)
        lax.fori_loop(0, 16, column_wait, 0)

    def exchange(stage, ref):
        @pl.when(y > 0)
        def _():
            border(stage, 0, ref.at[rows(3, 3)], ref.at[rows(19, 3)]).start()

        @pl.when(y < 3)
        def _():
            border(stage, 1, ref.at[rows(16, 3)], ref.at[rows(0, 3)]).start()

    def edges(src, dst, first):
        def body(k, c):
            for i in (first + 2 + k, 15 - first + k):
                dst[rows(i + 1, 1), :] = one(src, i)
            return c

        lax.fori_loop(0, 3, body, 0, unroll=3)

    def give(i):
        return remote(es.at[i], out.at[rows(i, 1), mine], g_send.at[i], g_recv.at[i], partner)

    def last_give(i, c):
        es[i] = one(s5, 8 * other + 2 + i)
        give(i).start()
        return c

    def last_keep(i, c):
        out[rows(i, 1), mine] = one(s5, 8 * zh + 2 + i)
        return c

    exchange(1, x2)
    sweep(x2, ya, 1, 15, 7)
    sweep(ya, yb, 2, 14, 6)
    sweep(yb, x3, 3, 13, 5)
    sweep(x3, s4, 4, 12, 8)
    sweep(s4, s5, 5, 11, 6)
    lax.fori_loop(0, 2, lambda k, c: last_give(6 * zh + k, c), 0, unroll=2)
    wait_borders(1, x2)
    edges(x2, ya, -2)
    edges(ya, yb, -1)
    edges(yb, x3, 0)
    exchange(2, x3)
    edges(x3, s4, 1)
    edges(s4, s5, 2)
    lax.fori_loop(0, 3, lambda k, c: last_give(2 + zh + k, c), 0, unroll=3)
    wait_borders(2, x3)
    edges(x3, s4, -2)
    edges(s4, s5, -1)
    lax.fori_loop(0, 3, lambda k, c: last_give(5 * other + k, c), 0, unroll=3)
    lax.fori_loop(0, 8, last_keep, 0, unroll=4)

    def finish(i, c):
        remote(es.at[i], out.at[rows(i, 1), theirs], g_send.at[i], g_recv.at[i], partner).wait()
        return c

    lax.fori_loop(0, 8, finish, 0)
    swap_edge.wait_send()
    swap_rest.wait_send()

    remote(op.at[0], op.at[0], o_send.at[0], o_recv.at[0], partner).wait_send()

    def share_end(k, c):
        remote(op.at[0], op.at[0], o_send.at[k], o_recv.at[0], partner).wait_send()
        return c

    lax.fori_loop(1, 8, share_end, 0)

    @pl.when(y > 0)
    def _():
        remote(op.at[pl.ds(2, 2)], op.at[pl.ds(18, 2)], o_send.at[9], o_recv.at[8], partner).wait_send()
        for stage in range(3):
            border(stage, 0, x1.at[rows(3, 3)], x1.at[rows(19, 3)]).wait_send()

    @pl.when(y < 3)
    def _():
        remote(op.at[pl.ds(16, 2)], op.at[pl.ds(0, 2)], o_send.at[10], o_recv.at[9], partner).wait_send()
        for stage in range(3):
            border(stage, 1, x1.at[rows(3, 3)], x1.at[rows(19, 3)]).wait_send()

    def sent(i, c):
        remote(ts.at[0], x2.at[rows(3, 1)], z_send.at[i], z_recv.at[0], partner).wait_send()
        return c

    lax.fori_loop(1, 16, sent, 0)

    @pl.when(jnp.logical_not(diagonal))
    def _():
        def gone(i, c):
            onward(i).wait_send()
            return c

        lax.fori_loop(0, 16, gone, 0)

    @pl.when(diagonal)
    def _():
        def passed(j, c):
            forward(j).wait_send()
            return c

        lax.fori_loop(0, 24, passed, 0)


def on_device(covariance, zonal, stencil):
    vmem, dma = pltpu.VMEM, pltpu.SemaphoreType.DMA
    return pl.pallas_call(
        kernel,
        out_shape=jax.ShapeDtypeStruct(covariance.shape, F32),
        in_specs=[pl.BlockSpec(memory_space=pltpu.VMEM)] * 3,
        out_specs=pl.BlockSpec(memory_space=pltpu.VMEM),
        scratch_shapes=[
            vmem((20, N + 8, N), F32),
            vmem((20, N, 2 * N), BF16),
            vmem((20, 3, N, N), F32),
            vmem((22 * N, N), F32),
            vmem((62 * N, N), F32),
            vmem((22 * N, N), F32),
            vmem((22 * N, N), F32),
            vmem((22 * N, N), F32),
            vmem((22 * N, N), F32),
            vmem((22 * N, N), F32),
            vmem((16, N, N), F32),
            vmem((8, N, N), F32),
            dma((2,)), dma((2,)), dma((11,)), dma((10,)), dma((6,)), dma((6,)),
            dma((16,)), dma((16,)), dma((16,)), dma((40,)), dma((24,)), dma((8,)), dma((8,)),
        ],
        compiler_params=pltpu.CompilerParams(
            collective_id=0, has_side_effects=True, vmem_limit_bytes=36 * 2**20),
        cost_estimate=pl.CostEstimate(flops=2_000_000_000, bytes_accessed=4 * 2**20, transcendentals=0),
        name="propagate",
    )(covariance, zonal, jnp.transpose(stencil, (1, 0, 2)))


def solution(mesh):
    placed = (P("rows", "cols"), P("rows", None, None), P("rows", None, None))
    return jax.shard_map(
        on_device, mesh=mesh, in_specs=placed, out_specs=P("rows", "cols"), check_vma=False
    )
```

```python
import jax
import jax.numpy as jnp
from jax import lax
from jax.experimental import pallas as pl
from jax.experimental.pallas import tpu as pltpu
from jax.sharding import PartitionSpec as P

MESH = pl.DeviceIdType.MESH
N = 128
F32, BF16 = jnp.float32, jnp.bfloat16


def div(a, b):
    return lax.div(a, jnp.int32(b))


def rem(a, b):
    return lax.rem(a, jnp.int32(b))


def device(x, y, z, core):
    return (y * 2 + div(z, 4), x * 8 + rem(z, 4) * 2 + core)


def rows(first, count):
    return pl.ds(pl.multiple_of(first * N, N), count * N)


def kernel(cov, zonal, stencil, out, st, op, z2, coef, x1, x2, x3, ya, yb, s4, s5, ts, es,
           l_sem, e_send, e_recv, o_send, o_recv, h_send, h_recv, z_send, z_recv, t_send, t_recv, f_send, g_send, g_recv):
    row, col = lax.axis_index("rows"), lax.axis_index("cols")
    y, zh = div(row, 2), rem(row, 2)
    x, zl, core = div(col, 8), div(rem(col, 8), 2), rem(col, 2)
    z = zh * 4 + zl
    me16 = z * 2 + core
    partner = (row + 1 - 2 * zh, col)
    piece = x * 2 + core
    other = 1 - zh
    diagonal = x == y

    def remote(src, dst, send, recv, dev):
        return pltpu.make_async_remote_copy(
            src_ref=src, dst_ref=dst, send_sem=send, recv_sem=recv, device_id=dev, device_id_type=MESH)

    theirs = pl.ds(pl.multiple_of(other * N, N), N)
    mine = pl.ds(pl.multiple_of(zh * N, N), N)
    load_stencil = pltpu.make_async_copy(stencil, st, l_sem.at[0])
    load_zonal = pltpu.make_async_copy(zonal, op.at[pl.ds(2 + 8 * zh, 8), 0:N, :], l_sem.at[1])
    load_own = pltpu.make_async_copy(cov.at[:, mine], x1.at[rows(3 + 8 * zh, 8)], l_sem.at[2])
    load_stencil.start()
    load_zonal.start()
    load_own.start()

    barrier = pltpu.get_barrier_semaphore()

    def greet(dev):
        pl.semaphore_signal(barrier, inc=1, device_id=dev, device_id_type=MESH)

    def greet_column(k, c):
        d = rem(me16 + k, 16)
        greet(device(x, y, div(d, 2), rem(d, 2)))
        return c

    lax.fori_loop(1, 16, greet_column, 0)

    def greet_group(k, c):
        q = rem(piece + k, 8)
        greet(device(div(q, 2), y, z, rem(q, 2)))
        return c

    lax.fori_loop(1, 8, greet_group, 0)

    @pl.when(y > 0)
    def _():
        greet(device(x, y - 1, z, core))

    @pl.when(y < 3)
    def _():
        greet(device(x, y + 1, z, core))

    @pl.when(diagonal)
    def _():
        for k in range(1, 4):
            greet(device(x, rem(x + k, 4), z, core))

    @pl.when(jnp.logical_not(diagonal))
    def _():
        greet(device(y, x, z, core))
        greet(device(y, y, z, core))

    load_stencil.wait()
    load_zonal.wait()
    for i in range(8):
        for part in range(3):
            op[2 + 8 * zh + i, N + part:N + part + 1, :] = st[part, i:i + 1, :]

    @pl.when(y == 0)
    def _():
        op[0:2] = jnp.zeros((2, N + 8, N), F32)
        for ref in (x1, x2, x3):
            ref[0:3 * N, :] = jnp.zeros((3 * N, N), F32)

    @pl.when(y == 3)
    def _():
        op[18:20] = jnp.zeros((2, N + 8, N), F32)
        for ref in (x1, x2, x3):
            ref[19 * N:22 * N, :] = jnp.zeros((3 * N, N), F32)

    writes = 15 + 7 + jnp.where(y > 0, 1, 0) + jnp.where(y < 3, 1, 0) + jnp.where(diagonal, 3, 2)
    pl.semaphore_wait(barrier, writes)

    swap_edge = remote(cov.at[rows(zh * 5, 3), theirs], x1.at[rows(3 + zh * 13, 3)],
                       e_send.at[0], e_recv.at[0], partner)
    swap_rest = remote(cov.at[rows(other * 3, 5), theirs], x1.at[rows(6 + zh * 5, 5)],
                       e_send.at[1], e_recv.at[1], partner)

    kept = 2 + 8 * zh + piece
    gotten = 2 + 8 * other + piece
    remote(op.at[kept], op.at[kept], o_send.at[0], o_recv.at[piece], partner).start()
    swap_edge.start()
    swap_rest.start()

    def border(stage, side, src, dst_first):
        dev = device(x, jnp.where(side == 0, y - 1, y + 1), z, core)
        return remote(src, dst_first, h_send.at[stage * 2 + side], h_recv.at[stage * 2 + side], dev)

    def has(side):
        return jnp.where(side == 0, y > 0, y < 3)

    @pl.when(has(zh))
    def _():
        border(0, zh, cov.at[rows(zh * 5, 3), mine], x1.at[rows(19 - 19 * zh, 3)]).start()

    def build(l, c):
        z_mat = op[l, 0:N, :]
        hi = z_mat.astype(BF16)
        z2[l, :, 0:N] = hi
        z2[l, :, N:2 * N] = (z_mat - hi.astype(F32)).astype(BF16)
        for part in range(3):
            coef[l, part] = jnp.broadcast_to(op[l, N + part:N + part + 1, :], (N, N)).T
        return c

    lax.fori_loop(2 + 8 * zh, 10 + 8 * zh, build, 0)

    remote(op.at[gotten], op.at[gotten], o_send.at[0], o_recv.at[piece], partner).wait_recv()

    def share(k, c):
        q = rem(piece + k, 8)
        remote(op.at[gotten], op.at[gotten], o_send.at[k], o_recv.at[piece], device(div(q, 2), y, z, rem(q, 2))).start()
        return c

    lax.fori_loop(1, 8, share, 0)

    def shared(k, c):
        q = rem(piece + k, 8)
        s = 2 + 8 * other + q
        remote(op.at[s], op.at[s], o_send.at[0], o_recv.at[q], partner).wait_recv()
        return c

    lax.fori_loop(1, 8, shared, 0)

    @pl.when(y > 0)
    def _():
        remote(op.at[pl.ds(2, 2)], op.at[pl.ds(18, 2)], o_send.at[9], o_recv.at[8],
               device(x, y - 1, z, core)).start()

    @pl.when(y < 3)
    def _():
        remote(op.at[pl.ds(16, 2)], op.at[pl.ds(0, 2)], o_send.at[10], o_recv.at[9],
               device(x, y + 1, z, core)).start()

    swap_edge.wait_recv()

    @pl.when(has(other))
    def _():
        border(0, other, x1.at[rows(3 + 13 * other, 3)], x1.at[rows(19 - 19 * other, 3)]).start()

    lax.fori_loop(2 + 8 * other, 10 + 8 * other, build, 0)

    @pl.when(y < 3)
    def _():
        remote(op.at[pl.ds(18, 2)], op.at[pl.ds(18, 2)], o_send.at[0], o_recv.at[8], partner).wait_recv()

    @pl.when(y > 0)
    def _():
        remote(op.at[pl.ds(0, 2)], op.at[pl.ds(0, 2)], o_send.at[0], o_recv.at[9], partner).wait_recv()

    lax.fori_loop(0, 2, build, 0)
    lax.fori_loop(18, 20, build, 0)

    def one(src, i):
        v = src[rows(i, 3), :]
        v = coef[i, 0] * v[N:2 * N] + coef[i, 1] * v[2 * N:] + coef[i, 2] * v[0:N]
        hi = v.astype(BF16)
        lo = (v - hi.astype(F32)).astype(BF16)
        right = jnp.concatenate(
            [jnp.concatenate([hi, hi], axis=0), jnp.concatenate([lo, jnp.zeros_like(lo)], axis=0)], axis=1)
        both = jnp.dot(z2[i], right, preferred_element_type=F32)
        return both[:, 0:N] + both[:, N:]

    def sweep(src, dst, first, last, unroll):
        def body(i, c):
            dst[rows(i + 1, 1), :] = one(src, i)
            return c

        lax.fori_loop(first + 2, last + 2, body, 0, unroll=unroll)

    def wait_borders(stage, ref):
        @pl.when(y < 3)
        def _():
            border(stage, 0, ref.at[rows(19, 3)], ref.at[rows(19, 3)]).wait_recv()

        @pl.when(y > 0)
        def _():
            border(stage, 1, ref.at[rows(0, 3)], ref.at[rows(0, 3)]).wait_recv()

    load_own.wait()
    swap_rest.wait_recv()
    wait_borders(0, x1)
    sweep(x1, ya, -2, 18, 5)
    sweep(ya, yb, -1, 17, 6)

    def turn(lat, c):
        ts[lat] = one(yb, lat + 2).T
        return c

    lax.fori_loop(0, 16, turn, 0, unroll=8)

    def order(i):
        return jnp.where(rem(i, 2) == 1, div(i + 1, 2), jnp.where(i == 0, 0, 16 - div(i, 2)))

    def block_of(d):
        zt = div(d, 2)
        return 8 * div(rem(zt, 4), 2) + 4 * rem(zt, 2) + 2 * rem(d, 2) + div(zt, 4)

    def place(s):
        return 3 + rem(div(s, 2), 4) * 4 + rem(s, 2) * 2 + div(s, 8)

    def landing(s):
        return rows(jnp.where(diagonal, place(s), 46 + s), 1)

    self_copy = pltpu.make_async_copy(ts.at[block_of(me16)], x2.at[landing(me16)], z_recv.at[me16])
    self_copy.start()

    def column_send(i, c):
        d = rem(me16 + order(i), 16)
        remote(ts.at[block_of(d)], x2.at[landing(me16)], z_send.at[i], z_recv.at[me16],
               device(x, y, div(d, 2), rem(d, 2))).start()
        return c

    lax.fori_loop(1, 16, column_send, 0)

    def source(i):
        return rem(me16 - order(i) + 16, 16)

    def column_wait(i, c):
        s = source(i)
        remote(ts.at[0], x2.at[landing(s)], z_send.at[0], z_recv.at[s], partner).wait_recv()
        return c

    def onward(i):
        s = source(i)
        relay = rem(i, 2) == 0
        slot = jnp.where(relay, 22 + rem(y + 3 - x, 4) * 8 + div(i, 2), place(s))
        sem = jnp.where(relay, 16 + rem(y + 3 - x, 4) * 8 + div(i, 2), s)
        return remote(x2.at[landing(s)], x2.at[rows(slot, 1)], t_send.at[i], t_recv.at[sem],
                      device(jnp.where(relay, x, y), x, z, core))

    def forward(j):
        m, o = div(j, 3), rem(j, 3)
        s = source(2 * m)
        return remote(x2.at[rows(22 + o * 8 + m, 1)], x2.at[rows(place(s), 1)], f_send.at[j], t_recv.at[s],
                      device(rem(x + 1 + o, 4), x, z, core))

    @pl.when(jnp.logical_not(diagonal))
    def _():
        def go(i, c):
            column_wait(i, 0)
            onward(i).start()
            return c

        lax.fori_loop(0, 16, go, 0)

        def arrive(s, c):
            remote(ts.at[0], x2.at[rows(place(s), 1)], z_send.at[0], t_recv.at[s], partner).wait_recv()
            return c

        lax.fori_loop(0, 16, arrive, 0)

    @pl.when(diagonal)
    def _():
        def pass_on(j, c):
            slot = rem(j, 3) * 8 + div(j, 3)
            remote(ts.at[0], x2.at[rows(22 + slot, 1)], z_send.at[0], t_recv.at[16 + slot], partner).wait_recv()
            forward(j).start()
            return c

        lax.fori_loop(0, 24, pass_on, 0)
        lax.fori_loop(0, 16, column_wait, 0)

    def exchange(stage, ref):
        @pl.when(y > 0)
        def _():
            border(stage, 0, ref.at[rows(3, 3)], ref.at[rows(19, 3)]).start()

        @pl.when(y < 3)
        def _():
            border(stage, 1, ref.at[rows(16, 3)], ref.at[rows(0, 3)]).start()

    def edges(src, dst, first):
        def body(k, c):
            for i in (first + 2 + k, 15 - first + k):
                dst[rows(i + 1, 1), :] = one(src, i)
            return c

        lax.fori_loop(0, 3, body, 0, unroll=3)

    def give(i):
        return remote(es.at[i], out.at[rows(i, 1), mine], g_send.at[i], g_recv.at[i], partner)

    def last_give(i, c):
        es[i] = one(s5, 8 * other + 2 + i)
        give(i).start()
        return c

    def last_keep(i, c):
        out[rows(i, 1), mine] = one(s5, 8 * zh + 2 + i)
        return c

    exchange(1, x2)
    sweep(x2, ya, 1, 15, 7)
    sweep(ya, yb, 2, 14, 6)
    sweep(yb, x3, 3, 13, 5)
    sweep(x3, s4, 4, 12, 8)
    sweep(s4, s5, 5, 11, 6)
    lax.fori_loop(0, 2, lambda k, c: last_give(6 * zh + k, c), 0, unroll=2)
    wait_borders(1, x2)
    edges(x2, ya, -2)
    edges(ya, yb, -1)
    edges(yb, x3, 0)
    exchange(2, x3)
    edges(x3, s4, 1)
    edges(s4, s5, 2)
    lax.fori_loop(0, 3, lambda k, c: last_give(2 + zh + k, c), 0, unroll=3)
    wait_borders(2, x3)
    edges(x3, s4, -2)
    edges(s4, s5, -1)
    lax.fori_loop(0, 3, lambda k, c: last_give(5 * other + k, c), 0, unroll=3)
    lax.fori_loop(0, 8, last_keep, 0, unroll=4)

    def finish(i, c):
        remote(es.at[i], out.at[rows(i, 1), theirs], g_send.at[i], g_recv.at[i], partner).wait()
        return c

    lax.fori_loop(0, 8, finish, 0)
    swap_edge.wait_send()
    swap_rest.wait_send()

    remote(op.at[0], op.at[0], o_send.at[0], o_recv.at[0], partner).wait_send()

    def share_end(k, c):
        remote(op.at[0], op.at[0], o_send.at[k], o_recv.at[0], partner).wait_send()
        return c

    lax.fori_loop(1, 8, share_end, 0)

    @pl.when(y > 0)
    def _():
        remote(op.at[pl.ds(2, 2)], op.at[pl.ds(18, 2)], o_send.at[9], o_recv.at[8], partner).wait_send()
        for stage in range(3):
            border(stage, 0, x1.at[rows(3, 3)], x1.at[rows(19, 3)]).wait_send()

    @pl.when(y < 3)
    def _():
        remote(op.at[pl.ds(16, 2)], op.at[pl.ds(0, 2)], o_send.at[10], o_recv.at[9], partner).wait_send()
        for stage in range(3):
            border(stage, 1, x1.at[rows(3, 3)], x1.at[rows(19, 3)]).wait_send()

    def sent(i, c):
        remote(ts.at[0], x2.at[rows(3, 1)], z_send.at[i], z_recv.at[0], partner).wait_send()
        return c

    lax.fori_loop(1, 16, sent, 0)

    @pl.when(jnp.logical_not(diagonal))
    def _():
        def gone(i, c):
            onward(i).wait_send()
            return c

        lax.fori_loop(0, 16, gone, 0)

    @pl.when(diagonal)
    def _():
        def passed(j, c):
            forward(j).wait_send()
            return c

        lax.fori_loop(0, 24, passed, 0)


def on_device(covariance, zonal, stencil):
    vmem, dma = pltpu.VMEM, pltpu.SemaphoreType.DMA
    return pl.pallas_call(
        kernel,
        out_shape=jax.ShapeDtypeStruct(covariance.shape, F32),
        in_specs=[pl.BlockSpec(memory_space=pltpu.HBM)] * 3,
        out_specs=pl.BlockSpec(memory_space=pltpu.VMEM),
        scratch_shapes=[
            vmem((3, 8, N), F32),
            vmem((20, N + 8, N), F32),
            vmem((20, N, 2 * N), BF16),
            vmem((20, 3, N, N), F32),
            vmem((22 * N, N), F32),
            vmem((62 * N, N), F32),
            vmem((22 * N, N), F32),
            vmem((22 * N, N), F32),
            vmem((22 * N, N), F32),
            vmem((22 * N, N), F32),
            vmem((22 * N, N), F32),
            vmem((16, N, N), F32),
            vmem((8, N, N), F32),
            dma((3,)), dma((2,)), dma((2,)), dma((11,)), dma((10,)), dma((6,)), dma((6,)),
            dma((16,)), dma((16,)), dma((16,)), dma((40,)), dma((24,)), dma((8,)), dma((8,)),
        ],
        compiler_params=pltpu.CompilerParams(
            collective_id=0, has_side_effects=True, vmem_limit_bytes=36 * 2**20),
        cost_estimate=pl.CostEstimate(flops=2_000_000_000, bytes_accessed=4 * 2**20, transcendentals=0),
        name="propagate",
    )(*(pltpu.with_memory_space_constraint(a, pltpu.HBM) for a in (covariance, zonal, jnp.transpose(stencil, (1, 0, 2)))))


def solution(mesh):
    placed = (P("rows", "cols"), P("rows", None, None), P("rows", None, None))
    return jax.shard_map(
        on_device, mesh=mesh, in_specs=placed, out_specs=P("rows", "cols"), check_vma=False
    )
```

```python
import jax
import jax.numpy as jnp
from jax import lax
from jax.experimental import pallas as pl
from jax.experimental.pallas import tpu as pltpu
from jax.sharding import PartitionSpec as P

MESH = pl.DeviceIdType.MESH
N = 128
F32, BF16 = jnp.float32, jnp.bfloat16


def div(a, b):
    return lax.div(a, jnp.int32(b))


def rem(a, b):
    return lax.rem(a, jnp.int32(b))


def device(x, y, z, core):
    return (y * 2 + div(z, 4), x * 8 + rem(z, 4) * 2 + core)


def rows(first, count):
    return pl.ds(pl.multiple_of(first * N, N), count * N)


def kernel(cov, zonal, stencil, out, st, op, z2, coef, x1, x2, x3, ya, yb, s4, s5, ts, es,
           l_sem, e_send, e_recv, o_send, o_recv, h_send, h_recv, z_send, z_recv, t_send, t_recv, f_send, g_send, g_recv):
    row, col = lax.axis_index("rows"), lax.axis_index("cols")
    y, zh = div(row, 2), rem(row, 2)
    x, zl, core = div(col, 8), div(rem(col, 8), 2), rem(col, 2)
    z = zh * 4 + zl
    me16 = z * 2 + core
    partner = (row + 1 - 2 * zh, col)
    piece = x * 2 + core
    other = 1 - zh
    diagonal = x == y

    def remote(src, dst, send, recv, dev):
        return pltpu.make_async_remote_copy(
            src_ref=src, dst_ref=dst, send_sem=send, recv_sem=recv, device_id=dev, device_id_type=MESH)

    theirs = pl.ds(pl.multiple_of(other * N, N), N)
    mine = pl.ds(pl.multiple_of(zh * N, N), N)
    load_stencil = pltpu.make_async_copy(stencil, st, l_sem.at[0])
    load_zonal = pltpu.make_async_copy(zonal, op.at[pl.ds(2 + 8 * zh, 8), 0:N, :], l_sem.at[1])
    load_own = pltpu.make_async_copy(cov.at[:, mine], x1.at[rows(3 + 8 * zh, 8)], l_sem.at[2])
    load_stencil.start()
    load_zonal.start()
    load_own.start()

    barrier = pltpu.get_barrier_semaphore()

    def greet(dev):
        pl.semaphore_signal(barrier, inc=1, device_id=dev, device_id_type=MESH)

    def greet_column(k, c):
        d = rem(me16 + k, 16)
        greet(device(x, y, div(d, 2), rem(d, 2)))
        return c

    lax.fori_loop(1, 16, greet_column, 0)

    def greet_group(k, c):
        q = rem(piece + k, 8)
        greet(device(div(q, 2), y, z, rem(q, 2)))
        return c

    lax.fori_loop(1, 8, greet_group, 0)

    @pl.when(y > 0)
    def _():
        greet(device(x, y - 1, z, core))

    @pl.when(y < 3)
    def _():
        greet(device(x, y + 1, z, core))

    @pl.when(diagonal)
    def _():
        for k in range(1, 4):
            greet(device(x, rem(x + k, 4), z, core))

    @pl.when(jnp.logical_not(diagonal))
    def _():
        greet(device(y, x, z, core))
        greet(device(y, y, z, core))

    load_stencil.wait()
    load_zonal.wait()
    for i in range(8):
        for part in range(3):
            op[2 + 8 * zh + i, N + part:N + part + 1, :] = st[part, i:i + 1, :]

    @pl.when(y == 0)
    def _():
        op[0:2] = jnp.zeros((2, N + 8, N), F32)
        for ref in (x1, x2, x3):
            ref[0:3 * N, :] = jnp.zeros((3 * N, N), F32)

    @pl.when(y == 3)
    def _():
        op[18:20] = jnp.zeros((2, N + 8, N), F32)
        for ref in (x1, x2, x3):
            ref[19 * N:22 * N, :] = jnp.zeros((3 * N, N), F32)

    writes = 15 + 7 + jnp.where(y > 0, 1, 0) + jnp.where(y < 3, 1, 0) + jnp.where(diagonal, 3, 2)
    pl.semaphore_wait(barrier, writes)

    swap_edge = remote(cov.at[rows(zh * 5, 3), theirs], x1.at[rows(3 + zh * 13, 3)],
                       e_send.at[0], e_recv.at[0], partner)
    swap_rest = remote(cov.at[rows(other * 3, 5), theirs], x1.at[rows(6 + zh * 5, 5)],
                       e_send.at[1], e_recv.at[1], partner)

    kept = 2 + 8 * zh + piece
    gotten = 2 + 8 * other + piece
    remote(op.at[kept], op.at[kept], o_send.at[0], o_recv.at[piece], partner).start()
    swap_edge.start()
    swap_rest.start()

    def border(stage, side, src, dst_first):
        dev = device(x, jnp.where(side == 0, y - 1, y + 1), z, core)
        return remote(src, dst_first, h_send.at[stage * 2 + side], h_recv.at[stage * 2 + side], dev)

    def has(side):
        return jnp.where(side == 0, y > 0, y < 3)

    @pl.when(has(zh))
    def _():
        border(0, zh, cov.at[rows(zh * 5, 3), mine], x1.at[rows(19 - 19 * zh, 3)]).start()

    def build(l, c):
        z_mat = op[l, 0:N, :]
        hi = z_mat.astype(BF16)
        z2[l, :, 0:N] = hi
        z2[l, :, N:2 * N] = (z_mat - hi.astype(F32)).astype(BF16)
        for part in range(3):
            coef[l, part] = jnp.broadcast_to(op[l, N + part:N + part + 1, :], (N, N)).T
        return c

    lax.fori_loop(2 + 8 * zh, 10 + 8 * zh, build, 0)

    remote(op.at[gotten], op.at[gotten], o_send.at[0], o_recv.at[piece], partner).wait_recv()

    def share(k, c):
        q = rem(piece + k, 8)
        remote(op.at[gotten], op.at[gotten], o_send.at[k], o_recv.at[piece], device(div(q, 2), y, z, rem(q, 2))).start()
        return c

    lax.fori_loop(1, 8, share, 0)

    def shared(k, c):
        q = rem(piece + k, 8)
        s = 2 + 8 * other + q
        remote(op.at[s], op.at[s], o_send.at[0], o_recv.at[q], partner).wait_recv()
        return c

    lax.fori_loop(1, 8, shared, 0)

    @pl.when(y > 0)
    def _():
        remote(op.at[pl.ds(2, 2)], op.at[pl.ds(18, 2)], o_send.at[9], o_recv.at[8],
               device(x, y - 1, z, core)).start()

    @pl.when(y < 3)
    def _():
        remote(op.at[pl.ds(16, 2)], op.at[pl.ds(0, 2)], o_send.at[10], o_recv.at[9],
               device(x, y + 1, z, core)).start()

    swap_edge.wait_recv()

    @pl.when(has(other))
    def _():
        border(0, other, x1.at[rows(3 + 13 * other, 3)], x1.at[rows(19 - 19 * other, 3)]).start()

    lax.fori_loop(2 + 8 * other, 10 + 8 * other, build, 0)

    @pl.when(y < 3)
    def _():
        remote(op.at[pl.ds(18, 2)], op.at[pl.ds(18, 2)], o_send.at[0], o_recv.at[8], partner).wait_recv()

    @pl.when(y > 0)
    def _():
        remote(op.at[pl.ds(0, 2)], op.at[pl.ds(0, 2)], o_send.at[0], o_recv.at[9], partner).wait_recv()

    lax.fori_loop(0, 2, build, 0)
    lax.fori_loop(18, 20, build, 0)

    def one(src, i):
        v = src[rows(i, 3), :]
        v = coef[i, 0] * v[N:2 * N] + coef[i, 1] * v[2 * N:] + coef[i, 2] * v[0:N]
        hi = v.astype(BF16)
        lo = (v - hi.astype(F32)).astype(BF16)
        right = jnp.concatenate(
            [jnp.concatenate([hi, hi], axis=0), jnp.concatenate([lo, jnp.zeros_like(lo)], axis=0)], axis=1)
        both = jnp.dot(z2[i], right, preferred_element_type=F32)
        return both[:, 0:N] + both[:, N:]

    def sweep(src, dst, first, last, unroll):
        def body(i, c):
            dst[rows(i + 1, 1), :] = one(src, i)
            return c

        lax.fori_loop(first + 2, last + 2, body, 0, unroll=unroll)

    def wait_borders(stage, ref):
        @pl.when(y < 3)
        def _():
            border(stage, 0, ref.at[rows(19, 3)], ref.at[rows(19, 3)]).wait_recv()

        @pl.when(y > 0)
        def _():
            border(stage, 1, ref.at[rows(0, 3)], ref.at[rows(0, 3)]).wait_recv()

    def order(i):
        return jnp.where(rem(i, 2) == 1, div(i + 1, 2), jnp.where(i == 0, 0, 16 - div(i, 2)))

    def block_of(d):
        zt = div(d, 2)
        return 8 * div(rem(zt, 4), 2) + 4 * rem(zt, 2) + 2 * rem(d, 2) + div(zt, 4)

    def place(s):
        return 3 + rem(div(s, 2), 4) * 4 + rem(s, 2) * 2 + div(s, 8)

    def landing(s):
        return rows(jnp.where(diagonal, place(s), 46 + s), 1)

    def place_of(lat):
        return (4 * rem(lat, 2) + 2 * div(lat, 8) + rem(div(lat, 4), 2)) * 2 + rem(div(lat, 2), 2)

    def column_send(lat, c):
        d = place_of(lat)

        @pl.when(d == me16)
        def _():
            pltpu.make_async_copy(ts.at[lat], x2.at[landing(me16)], z_recv.at[me16]).start()

        @pl.when(d != me16)
        def _():
            remote(ts.at[lat], x2.at[landing(me16)], z_send.at[lat], z_recv.at[me16],
                   device(x, y, div(d, 2), rem(d, 2))).start()

        return c

    def span(src, dst, first, count):
        def body(k, c):
            dst[rows(first + k + 1, 1), :] = one(src, first + k)
            return c

        lax.fori_loop(0, count, body, 0, unroll=count)

    def turn(first, count):
        def body(k, c):
            ts[first - 2 + k] = one(yb, first + k).T
            return c

        lax.fori_loop(0, count, body, 0, unroll=count)

    def wait_border(side):
        border(0, side, x1.at[rows(19 - 19 * side, 3)], x1.at[rows(19 - 19 * side, 3)]).wait_recv()

    load_own.wait()

    @pl.when(has(zh))
    def _():
        wait_border(other)

    span(x1, ya, 11 * zh, 9)
    span(ya, yb, 1 + 11 * zh, 7)
    turn(2 + 11 * zh, 5)

    swap_rest.wait_recv()

    @pl.when(has(other))
    def _():
        wait_border(zh)

    span(x1, ya, 9 * other, 11)
    span(ya, yb, 1 + 7 * other, 11)
    turn(2 + 5 * other, 11)

    def remaining(i, c):
        return column_send(block_of(rem(me16 + order(i), 16)), c)

    lax.fori_loop(0, 16, remaining, 0)

    def source(i):
        return rem(me16 - order(i) + 16, 16)

    def column_wait(i, c):
        s = source(i)
        remote(ts.at[0], x2.at[landing(s)], z_send.at[0], z_recv.at[s], partner).wait_recv()
        return c

    def onward(i):
        s = source(i)
        relay = rem(i, 2) == 0
        slot = jnp.where(relay, 22 + rem(y + 3 - x, 4) * 8 + div(i, 2), place(s))
        sem = jnp.where(relay, 16 + rem(y + 3 - x, 4) * 8 + div(i, 2), s)
        return remote(x2.at[landing(s)], x2.at[rows(slot, 1)], t_send.at[i], t_recv.at[sem],
                      device(jnp.where(relay, x, y), x, z, core))

    def forward(j):
        m, o = div(j, 3), rem(j, 3)
        s = source(2 * m)
        return remote(x2.at[rows(22 + o * 8 + m, 1)], x2.at[rows(place(s), 1)], f_send.at[j], t_recv.at[s],
                      device(rem(x + 1 + o, 4), x, z, core))

    @pl.when(jnp.logical_not(diagonal))
    def _():
        def go(i, c):
            column_wait(i, 0)
            onward(i).start()
            return c

        lax.fori_loop(0, 16, go, 0)

        def arrive(s, c):
            remote(ts.at[0], x2.at[rows(place(s), 1)], z_send.at[0], t_recv.at[s], partner).wait_recv()
            return c

        lax.fori_loop(0, 16, arrive, 0)

    @pl.when(diagonal)
    def _():
        def pass_on(j, c):
            slot = rem(j, 3) * 8 + div(j, 3)
            remote(ts.at[0], x2.at[rows(22 + slot, 1)], z_send.at[0], t_recv.at[16 + slot], partner).wait_recv()
            forward(j).start()
            return c

        lax.fori_loop(0, 24, pass_on, 0)
        lax.fori_loop(0, 16, column_wait, 0)

    def exchange(stage, ref):
        @pl.when(y > 0)
        def _():
            border(stage, 0, ref.at[rows(3, 3)], ref.at[rows(19, 3)]).start()

        @pl.when(y < 3)
        def _():
            border(stage, 1, ref.at[rows(16, 3)], ref.at[rows(0, 3)]).start()

    def edges(src, dst, first):
        def body(k, c):
            for i in (first + 2 + k, 15 - first + k):
                dst[rows(i + 1, 1), :] = one(src, i)
            return c

        lax.fori_loop(0, 3, body, 0, unroll=3)

    def give(i):
        return remote(es.at[i], out.at[rows(i, 1), mine], g_send.at[i], g_recv.at[i], partner)

    def last_give(i, c):
        es[i] = one(s5, 8 * other + 2 + i)
        give(i).start()
        return c

    def last_keep(i, c):
        out[rows(i, 1), mine] = one(s5, 8 * zh + 2 + i)
        return c

    exchange(1, x2)
    sweep(x2, ya, 1, 15, 7)
    sweep(ya, yb, 2, 14, 6)
    sweep(yb, x3, 3, 13, 5)
    sweep(x3, s4, 4, 12, 8)
    sweep(s4, s5, 5, 11, 6)
    lax.fori_loop(0, 2, lambda k, c: last_give(6 * zh + k, c), 0, unroll=2)
    wait_borders(1, x2)
    edges(x2, ya, -2)
    edges(ya, yb, -1)
    edges(yb, x3, 0)
    exchange(2, x3)
    edges(x3, s4, 1)
    edges(s4, s5, 2)
    lax.fori_loop(0, 3, lambda k, c: last_give(2 + zh + k, c), 0, unroll=3)
    wait_borders(2, x3)
    edges(x3, s4, -2)
    edges(s4, s5, -1)
    lax.fori_loop(0, 3, lambda k, c: last_give(5 * other + k, c), 0, unroll=3)
    lax.fori_loop(0, 8, last_keep, 0, unroll=4)

    def finish(i, c):
        remote(es.at[i], out.at[rows(i, 1), theirs], g_send.at[i], g_recv.at[i], partner).wait()
        return c

    lax.fori_loop(0, 8, finish, 0)
    swap_edge.wait_send()
    swap_rest.wait_send()

    remote(op.at[0], op.at[0], o_send.at[0], o_recv.at[0], partner).wait_send()

    def share_end(k, c):
        remote(op.at[0], op.at[0], o_send.at[k], o_recv.at[0], partner).wait_send()
        return c

    lax.fori_loop(1, 8, share_end, 0)

    @pl.when(y > 0)
    def _():
        remote(op.at[pl.ds(2, 2)], op.at[pl.ds(18, 2)], o_send.at[9], o_recv.at[8], partner).wait_send()
        for stage in range(3):
            border(stage, 0, x1.at[rows(3, 3)], x1.at[rows(19, 3)]).wait_send()

    @pl.when(y < 3)
    def _():
        remote(op.at[pl.ds(16, 2)], op.at[pl.ds(0, 2)], o_send.at[10], o_recv.at[9], partner).wait_send()
        for stage in range(3):
            border(stage, 1, x1.at[rows(3, 3)], x1.at[rows(19, 3)]).wait_send()

    def sent(lat, c):
        @pl.when(place_of(lat) != me16)
        def _():
            remote(ts.at[0], x2.at[rows(3, 1)], z_send.at[lat], z_recv.at[0], partner).wait_send()

        return c

    lax.fori_loop(0, 16, sent, 0)

    @pl.when(jnp.logical_not(diagonal))
    def _():
        def gone(i, c):
            onward(i).wait_send()
            return c

        lax.fori_loop(0, 16, gone, 0)

    @pl.when(diagonal)
    def _():
        def passed(j, c):
            forward(j).wait_send()
            return c

        lax.fori_loop(0, 24, passed, 0)


def on_device(covariance, zonal, stencil):
    vmem, dma = pltpu.VMEM, pltpu.SemaphoreType.DMA
    return pl.pallas_call(
        kernel,
        out_shape=jax.ShapeDtypeStruct(covariance.shape, F32),
        in_specs=[pl.BlockSpec(memory_space=pltpu.HBM)] * 3,
        out_specs=pl.BlockSpec(memory_space=pltpu.VMEM),
        scratch_shapes=[
            vmem((3, 8, N), F32),
            vmem((20, N + 8, N), F32),
            vmem((20, N, 2 * N), BF16),
            vmem((20, 3, N, N), F32),
            vmem((22 * N, N), F32),
            vmem((62 * N, N), F32),
            vmem((22 * N, N), F32),
            vmem((22 * N, N), F32),
            vmem((22 * N, N), F32),
            vmem((22 * N, N), F32),
            vmem((22 * N, N), F32),
            vmem((16, N, N), F32),
            vmem((8, N, N), F32),
            dma((3,)), dma((2,)), dma((2,)), dma((11,)), dma((10,)), dma((6,)), dma((6,)),
            dma((16,)), dma((16,)), dma((16,)), dma((40,)), dma((24,)), dma((8,)), dma((8,)),
        ],
        compiler_params=pltpu.CompilerParams(
            collective_id=0, has_side_effects=True, vmem_limit_bytes=36 * 2**20),
        cost_estimate=pl.CostEstimate(flops=2_000_000_000, bytes_accessed=4 * 2**20, transcendentals=0),
        name="propagate",
    )(*(pltpu.with_memory_space_constraint(a, pltpu.HBM) for a in (covariance, zonal, jnp.transpose(stencil, (1, 0, 2)))))


def solution(mesh):
    placed = (P("rows", "cols"), P("rows", None, None), P("rows", None, None))
    return jax.shard_map(
        on_device, mesh=mesh, in_specs=placed, out_specs=P("rows", "cols"), check_vma=False
    )
```

```python
import jax
import jax.numpy as jnp
from jax import lax
from jax.experimental import pallas as pl
from jax.experimental.pallas import tpu as pltpu
from jax.sharding import PartitionSpec as P

MESH = pl.DeviceIdType.MESH
N = 128
F32, BF16 = jnp.float32, jnp.bfloat16


def div(a, b):
    return lax.div(a, jnp.int32(b))


def rem(a, b):
    return lax.rem(a, jnp.int32(b))


def device(x, y, z, core):
    return (y * 2 + div(z, 4), x * 8 + rem(z, 4) * 2 + core)


def rows(first, count):
    return pl.ds(pl.multiple_of(first * N, N), count * N)


def kernel(cov, zonal, stencil, out, st, op, z2, coef, x1, x2, x3, ya, yb, s4, s5, ts, es,
           l_sem, e_send, e_recv, o_send, o_recv, h_send, h_recv, z_send, z_recv, t_send, t_recv, f_send, g_send, g_recv):
    row, col = lax.axis_index("rows"), lax.axis_index("cols")
    y, zh = div(row, 2), rem(row, 2)
    x, zl, core = div(col, 8), div(rem(col, 8), 2), rem(col, 2)
    z = zh * 4 + zl
    me16 = z * 2 + core
    partner = (row + 1 - 2 * zh, col)
    piece = x * 2 + core
    other = 1 - zh
    diagonal = x == y
    near = rem(x + y, 2) == 1

    def remote(src, dst, send, recv, dev):
        return pltpu.make_async_remote_copy(
            src_ref=src, dst_ref=dst, send_sem=send, recv_sem=recv, device_id=dev, device_id_type=MESH)

    theirs = pl.ds(pl.multiple_of(other * N, N), N)
    mine = pl.ds(pl.multiple_of(zh * N, N), N)
    load_stencil = pltpu.make_async_copy(stencil, st, l_sem.at[0])
    load_zonal = pltpu.make_async_copy(zonal, op.at[pl.ds(2 + 8 * zh, 8), 0:N, :], l_sem.at[1])
    load_own = pltpu.make_async_copy(cov.at[:, mine], x1.at[rows(3 + 8 * zh, 8)], l_sem.at[2])
    load_stencil.start()
    load_zonal.start()
    load_own.start()

    barrier = pltpu.get_barrier_semaphore()

    def greet(dev):
        pl.semaphore_signal(barrier, inc=1, device_id=dev, device_id_type=MESH)

    def greet_column(k, c):
        d = rem(me16 + k, 16)
        greet(device(x, y, div(d, 2), rem(d, 2)))
        return c

    lax.fori_loop(1, 16, greet_column, 0)

    def greet_group(k, c):
        q = rem(piece + k, 8)
        greet(device(div(q, 2), y, z, rem(q, 2)))
        return c

    lax.fori_loop(1, 8, greet_group, 0)

    @pl.when(y > 0)
    def _():
        greet(device(x, y - 1, z, core))

    @pl.when(y < 3)
    def _():
        greet(device(x, y + 1, z, core))

    @pl.when(diagonal)
    def _():
        for k in (1, 3):
            greet(device(x, rem(x + k, 4), z, core))

    @pl.when(jnp.logical_not(diagonal))
    def _():
        greet(device(y, jnp.where(near, y, x), z, core))

    load_stencil.wait()
    load_zonal.wait()
    for i in range(8):
        for part in range(3):
            op[2 + 8 * zh + i, N + part:N + part + 1, :] = st[part, i:i + 1, :]

    @pl.when(y == 0)
    def _():
        op[0:2] = jnp.zeros((2, N + 8, N), F32)
        for ref in (x1, x2, x3):
            ref[0:3 * N, :] = jnp.zeros((3 * N, N), F32)

    @pl.when(y == 3)
    def _():
        op[18:20] = jnp.zeros((2, N + 8, N), F32)
        for ref in (x1, x2, x3):
            ref[19 * N:22 * N, :] = jnp.zeros((3 * N, N), F32)

    writes = 15 + 7 + jnp.where(y > 0, 1, 0) + jnp.where(y < 3, 1, 0) + jnp.where(diagonal, 2, 1)
    pl.semaphore_wait(barrier, writes)

    swap_edge = remote(cov.at[rows(zh * 5, 3), theirs], x1.at[rows(3 + zh * 13, 3)],
                       e_send.at[0], e_recv.at[0], partner)
    swap_rest = remote(cov.at[rows(other * 3, 5), theirs], x1.at[rows(6 + zh * 5, 5)],
                       e_send.at[1], e_recv.at[1], partner)

    kept = 2 + 8 * zh + piece
    gotten = 2 + 8 * other + piece
    remote(op.at[kept], op.at[kept], o_send.at[0], o_recv.at[piece], partner).start()
    swap_edge.start()
    swap_rest.start()

    def border(stage, side, src, dst_first):
        dev = device(x, jnp.where(side == 0, y - 1, y + 1), z, core)
        return remote(src, dst_first, h_send.at[stage * 2 + side], h_recv.at[stage * 2 + side], dev)

    def has(side):
        return jnp.where(side == 0, y > 0, y < 3)

    @pl.when(has(zh))
    def _():
        border(0, zh, cov.at[rows(zh * 5, 3), mine], x1.at[rows(19 - 19 * zh, 3)]).start()

    def build(l, c):
        z_mat = op[l, 0:N, :]
        hi = z_mat.astype(BF16)
        z2[l, :, 0:N] = hi
        z2[l, :, N:2 * N] = (z_mat - hi.astype(F32)).astype(BF16)
        for part in range(3):
            coef[l, part] = jnp.broadcast_to(op[l, N + part:N + part + 1, :], (N, N)).T
        return c

    lax.fori_loop(2 + 8 * zh, 10 + 8 * zh, build, 0)

    remote(op.at[gotten], op.at[gotten], o_send.at[0], o_recv.at[piece], partner).wait_recv()

    def share(k, c):
        q = rem(piece + k, 8)
        remote(op.at[gotten], op.at[gotten], o_send.at[k], o_recv.at[piece], device(div(q, 2), y, z, rem(q, 2))).start()
        return c

    lax.fori_loop(1, 8, share, 0)

    def shared(k, c):
        q = rem(piece + k, 8)
        s = 2 + 8 * other + q
        remote(op.at[s], op.at[s], o_send.at[0], o_recv.at[q], partner).wait_recv()
        return c

    lax.fori_loop(1, 8, shared, 0)

    @pl.when(y > 0)
    def _():
        remote(op.at[pl.ds(2, 2)], op.at[pl.ds(18, 2)], o_send.at[9], o_recv.at[8],
               device(x, y - 1, z, core)).start()

    @pl.when(y < 3)
    def _():
        remote(op.at[pl.ds(16, 2)], op.at[pl.ds(0, 2)], o_send.at[10], o_recv.at[9],
               device(x, y + 1, z, core)).start()

    swap_edge.wait_recv()

    @pl.when(has(other))
    def _():
        border(0, other, x1.at[rows(3 + 13 * other, 3)], x1.at[rows(19 - 19 * other, 3)]).start()

    lax.fori_loop(2 + 8 * other, 10 + 8 * other, build, 0)

    @pl.when(y < 3)
    def _():
        remote(op.at[pl.ds(18, 2)], op.at[pl.ds(18, 2)], o_send.at[0], o_recv.at[8], partner).wait_recv()

    @pl.when(y > 0)
    def _():
        remote(op.at[pl.ds(0, 2)], op.at[pl.ds(0, 2)], o_send.at[0], o_recv.at[9], partner).wait_recv()

    lax.fori_loop(0, 2, build, 0)
    lax.fori_loop(18, 20, build, 0)

    def one(src, i):
        v = src[rows(i, 3), :]
        v = coef[i, 0] * v[N:2 * N] + coef[i, 1] * v[2 * N:] + coef[i, 2] * v[0:N]
        hi = v.astype(BF16)
        lo = (v - hi.astype(F32)).astype(BF16)
        right = jnp.concatenate(
            [jnp.concatenate([hi, hi], axis=0), jnp.concatenate([lo, jnp.zeros_like(lo)], axis=0)], axis=1)
        both = jnp.dot(z2[i], right, preferred_element_type=F32)
        return both[:, 0:N] + both[:, N:]

    def sweep(src, dst, first, last, unroll):
        def body(i, c):
            dst[rows(i + 1, 1), :] = one(src, i)
            return c

        lax.fori_loop(first + 2, last + 2, body, 0, unroll=unroll)

    def wait_borders(stage, ref):
        @pl.when(y < 3)
        def _():
            border(stage, 0, ref.at[rows(19, 3)], ref.at[rows(19, 3)]).wait_recv()

        @pl.when(y > 0)
        def _():
            border(stage, 1, ref.at[rows(0, 3)], ref.at[rows(0, 3)]).wait_recv()

    def order(i):
        return jnp.where(rem(i, 2) == 1, div(i + 1, 2), jnp.where(i == 0, 0, 16 - div(i, 2)))

    def block_of(d):
        zt = div(d, 2)
        return 8 * div(rem(zt, 4), 2) + 4 * rem(zt, 2) + 2 * rem(d, 2) + div(zt, 4)

    def place(s):
        return 3 + rem(div(s, 2), 4) * 4 + rem(s, 2) * 2 + div(s, 8)

    def landing(s):
        return rows(jnp.where(diagonal, place(s), 54 + s), 1)

    def place_of(lat):
        return (4 * rem(lat, 2) + 2 * div(lat, 8) + rem(div(lat, 4), 2)) * 2 + rem(div(lat, 2), 2)

    def column_send(lat, c):
        d = place_of(lat)

        @pl.when(d == me16)
        def _():
            pltpu.make_async_copy(ts.at[lat], x2.at[landing(me16)], z_recv.at[me16]).start()

        @pl.when(d != me16)
        def _():
            remote(ts.at[lat], x2.at[landing(me16)], z_send.at[lat], z_recv.at[me16],
                   device(x, y, div(d, 2), rem(d, 2))).start()

        return c

    def span(src, dst, first, count):
        def body(k, c):
            dst[rows(first + k + 1, 1), :] = one(src, first + k)
            return c

        lax.fori_loop(0, count, body, 0, unroll=count)

    def turn(first, count):
        def body(k, c):
            ts[first - 2 + k] = one(yb, first + k).T
            return c

        lax.fori_loop(0, count, body, 0, unroll=count)

    def wait_border(side):
        border(0, side, x1.at[rows(19 - 19 * side, 3)], x1.at[rows(19 - 19 * side, 3)]).wait_recv()

    load_own.wait()

    @pl.when(has(zh))
    def _():
        wait_border(other)

    span(x1, ya, 11 * zh, 9)
    span(ya, yb, 1 + 11 * zh, 7)
    turn(2 + 11 * zh, 5)

    swap_rest.wait_recv()

    @pl.when(has(other))
    def _():
        wait_border(zh)

    span(x1, ya, 9 * other, 11)
    span(ya, yb, 1 + 7 * other, 11)
    turn(2 + 5 * other, 11)

    def remaining(i, c):
        return column_send(block_of(rem(me16 + order(i), 16)), c)

    lax.fori_loop(0, 16, remaining, 0)

    def source(i):
        return rem(me16 - order(i) + 16, 16)

    def column_wait(i, c):
        s = source(i)
        remote(ts.at[0], x2.at[landing(s)], z_send.at[0], z_recv.at[s], partner).wait_recv()
        return c

    def onward(i):
        s = source(i)
        way = div(rem(y + 3 - x, 4), 2) * 16 + i
        slot = jnp.where(near, 22 + way, place(s))
        sem = jnp.where(near, 16 + way, s)
        return remote(x2.at[landing(s)], x2.at[rows(slot, 1)], t_send.at[i], t_recv.at[sem],
                      device(jnp.where(near, x, y), x, z, core))

    def forward(j):
        i, o = div(j, 2), rem(j, 2)
        s = source(i)
        return remote(x2.at[rows(22 + o * 16 + i, 1)], x2.at[rows(place(s), 1)], f_send.at[j], t_recv.at[s],
                      device(rem(x + 1 + 2 * o, 4), x, z, core))

    @pl.when(jnp.logical_not(diagonal))
    def _():
        def go(i, c):
            column_wait(i, 0)
            onward(i).start()
            return c

        lax.fori_loop(0, 16, go, 0)

        def arrive(s, c):
            remote(ts.at[0], x2.at[rows(place(s), 1)], z_send.at[0], t_recv.at[s], partner).wait_recv()
            return c

        lax.fori_loop(0, 16, arrive, 0)

    @pl.when(diagonal)
    def _():
        def pass_on(j, c):
            slot = rem(j, 2) * 16 + div(j, 2)
            remote(ts.at[0], x2.at[rows(22 + slot, 1)], z_send.at[0], t_recv.at[16 + slot], partner).wait_recv()
            forward(j).start()
            return c

        lax.fori_loop(0, 32, pass_on, 0)
        lax.fori_loop(0, 16, column_wait, 0)

    def exchange(stage, ref):
        @pl.when(y > 0)
        def _():
            border(stage, 0, ref.at[rows(3, 3)], ref.at[rows(19, 3)]).start()

        @pl.when(y < 3)
        def _():
            border(stage, 1, ref.at[rows(16, 3)], ref.at[rows(0, 3)]).start()

    def edges(src, dst, first):
        def body(k, c):
            for i in (first + 2 + k, 15 - first + k):
                dst[rows(i + 1, 1), :] = one(src, i)
            return c

        lax.fori_loop(0, 3, body, 0, unroll=3)

    def give(i):
        return remote(es.at[i], out.at[rows(i, 1), mine], g_send.at[i], g_recv.at[i], partner)

    def last_give(i, c):
        es[i] = one(s5, 8 * other + 2 + i)
        give(i).start()
        return c

    def last_keep(i, c):
        out[rows(i, 1), mine] = one(s5, 8 * zh + 2 + i)
        return c

    exchange(1, x2)
    sweep(x2, ya, 1, 15, 7)
    sweep(ya, yb, 2, 14, 6)
    sweep(yb, x3, 3, 13, 5)
    sweep(x3, s4, 4, 12, 8)
    sweep(s4, s5, 5, 11, 6)
    lax.fori_loop(0, 2, lambda k, c: last_give(6 * zh + k, c), 0, unroll=2)
    wait_borders(1, x2)
    edges(x2, ya, -2)
    edges(ya, yb, -1)
    edges(yb, x3, 0)
    exchange(2, x3)
    edges(x3, s4, 1)
    edges(s4, s5, 2)
    lax.fori_loop(0, 3, lambda k, c: last_give(2 + zh + k, c), 0, unroll=3)
    wait_borders(2, x3)
    edges(x3, s4, -2)
    edges(s4, s5, -1)
    lax.fori_loop(0, 3, lambda k, c: last_give(5 * other + k, c), 0, unroll=3)
    lax.fori_loop(0, 8, last_keep, 0, unroll=4)

    def finish(i, c):
        remote(es.at[i], out.at[rows(i, 1), theirs], g_send.at[i], g_recv.at[i], partner).wait()
        return c

    lax.fori_loop(0, 8, finish, 0)
    swap_edge.wait_send()
    swap_rest.wait_send()

    remote(op.at[0], op.at[0], o_send.at[0], o_recv.at[0], partner).wait_send()

    def share_end(k, c):
        remote(op.at[0], op.at[0], o_send.at[k], o_recv.at[0], partner).wait_send()
        return c

    lax.fori_loop(1, 8, share_end, 0)

    @pl.when(y > 0)
    def _():
        remote(op.at[pl.ds(2, 2)], op.at[pl.ds(18, 2)], o_send.at[9], o_recv.at[8], partner).wait_send()
        for stage in range(3):
            border(stage, 0, x1.at[rows(3, 3)], x1.at[rows(19, 3)]).wait_send()

    @pl.when(y < 3)
    def _():
        remote(op.at[pl.ds(16, 2)], op.at[pl.ds(0, 2)], o_send.at[10], o_recv.at[9], partner).wait_send()
        for stage in range(3):
            border(stage, 1, x1.at[rows(3, 3)], x1.at[rows(19, 3)]).wait_send()

    def sent(lat, c):
        @pl.when(place_of(lat) != me16)
        def _():
            remote(ts.at[0], x2.at[rows(3, 1)], z_send.at[lat], z_recv.at[0], partner).wait_send()

        return c

    lax.fori_loop(0, 16, sent, 0)

    @pl.when(jnp.logical_not(diagonal))
    def _():
        def gone(i, c):
            onward(i).wait_send()
            return c

        lax.fori_loop(0, 16, gone, 0)

    @pl.when(diagonal)
    def _():
        def passed(j, c):
            forward(j).wait_send()
            return c

        lax.fori_loop(0, 32, passed, 0)


def on_device(covariance, zonal, stencil):
    vmem, dma = pltpu.VMEM, pltpu.SemaphoreType.DMA
    return pl.pallas_call(
        kernel,
        out_shape=jax.ShapeDtypeStruct(covariance.shape, F32),
        in_specs=[pl.BlockSpec(memory_space=pltpu.HBM)] * 3,
        out_specs=pl.BlockSpec(memory_space=pltpu.VMEM),
        scratch_shapes=[
            vmem((3, 8, N), F32),
            vmem((20, N + 8, N), F32),
            vmem((20, N, 2 * N), BF16),
            vmem((20, 3, N, N), F32),
            vmem((22 * N, N), F32),
            vmem((70 * N, N), F32),
            vmem((22 * N, N), F32),
            vmem((22 * N, N), F32),
            vmem((22 * N, N), F32),
            vmem((22 * N, N), F32),
            vmem((22 * N, N), F32),
            vmem((16, N, N), F32),
            vmem((8, N, N), F32),
            dma((3,)), dma((2,)), dma((2,)), dma((11,)), dma((10,)), dma((6,)), dma((6,)),
            dma((16,)), dma((16,)), dma((16,)), dma((48,)), dma((32,)), dma((8,)), dma((8,)),
        ],
        compiler_params=pltpu.CompilerParams(
            collective_id=0, has_side_effects=True, vmem_limit_bytes=36 * 2**20),
        cost_estimate=pl.CostEstimate(flops=2_000_000_000, bytes_accessed=4 * 2**20, transcendentals=0),
        name="propagate",
    )(*(pltpu.with_memory_space_constraint(a, pltpu.HBM) for a in (covariance, zonal, jnp.transpose(stencil, (1, 0, 2)))))


def solution(mesh):
    placed = (P("rows", "cols"), P("rows", None, None), P("rows", None, None))
    return jax.shard_map(
        on_device, mesh=mesh, in_specs=placed, out_specs=P("rows", "cols"), check_vma=False
    )
```
